32 devices in a mesh: il: 16 (over z, y, core), xl: 2 (over x).
Axes of the slice: x: 2, y: 2, z: 4, core: 2. Of those that a mesh axis runs over, the one named last changes fastest.
Arguments:
- solution: float32 [64, 128, 512], P('il', 'xl'), may hold values from -6 to 6
- residual: float32 [64, 128, 512], P('il', 'xl'), may hold values from -30 to 30
- direction: float32 [64, 128, 512], P('il', 'xl'), may hold values from -30 to 30
- slope_il: float32 [64, 128, 512], P('il', 'xl'), may hold values from -1.5 to 1.5
- slope_xl: float32 [64, 128, 512], P('il', 'xl'), may hold values from -1.5 to 1.5
- weights: float32 [64, 128, 512], P('il', 'xl'), may hold values from 0.2 to 1
Outputs:
- new_solution: float32 [64, 128, 512], P('il', 'xl')
- new_residual: float32 [64, 128, 512], P('il', 'xl')
- new_direction: float32 [64, 128, 512], P('il', 'xl')
The draws below stay inside these ranges and needn't reach their ends.
All inputs are finite; a program needn't handle non-finite values.
Results may differ from the reference program's by a relative error of at most 0.00002.
Values sent between devices are 32-bit elements; how exact they have to be, the bound alone decides.
No kernel may reach another device: no remote copies, remote signals or barrier semaphores. Data moves between devices by JAX's collectives and lax.ppermute only.
A program may use at most 64 MiB of HBM per device.

```python
import jax
import jax.numpy as jnp

NT = 512
NI = 64
NX = 128


def rising_field(key, salt):
    keys = jax.random.split(jax.random.fold_in(key, salt), 1)
    inline = jnp.arange(NI, dtype=jnp.float32)[:, None, None]
    ramp = jnp.sqrt(3.0) ** (inline / max(NI - 1, 1))
    base = jnp.clip(jax.random.normal(keys[0], (NI, NX, NT), jnp.float32), -6.0, 6.0)
    return (ramp * base).astype(jnp.float32)


def draw_residual(key, part):
    return rising_field(key, 11)


def draw_direction(key, part):
    return rising_field(key, 23)


def levels(rng, extent, shards, smallest, largest):
    loudness, own = 1.0, jax.random.fold_in(rng, 6)
    for axis_at, parts in shards:
        heights = jnp.exp(jax.random.uniform(jax.random.fold_in(own, axis_at), (parts,), jnp.float32, smallest / len(shards), largest / len(shards)))
        loudness = loudness * jnp.repeat(heights, extent[axis_at] // parts).reshape([-1 if axis == axis_at else 1 for axis in range(len(extent))])
    return loudness


def bell_draw(own_key, shape, deviation, most, shards=(), kind=jnp.bfloat16):
    values = jax.random.normal(own_key, shape, jnp.float32) * deviation
    if len(shards) > 0:
        values = levels(own_key, shape, shards, -0.22, 0.18) * values
    return jnp.clip(values, min=-most, max=most).astype(kind)


def setup_inputs(seed: int = 0) -> dict:
    key_list = jax.random.split(jax.random.key(seed), 7)
    solution = bell_draw(key_list[0], (NI, NX, NT), 1.0, 6.0, ((0, 16), (1, 2)), jnp.float32)
    residual = draw_residual(jax.random.fold_in(key_list[6], 71), 0)
    direction = draw_direction(jax.random.fold_in(key_list[6], 71), 0)
    slope_il = jnp.clip(jax.random.uniform(key_list[3], (NI, NX, NT), jnp.float32, -1.5, 1.5) * levels(key_list[3], (NI, NX, NT), ((0, 16), (1, 2)), -0.4, 0.0), -1.5, 1.5)
    slope_xl = jnp.clip(jax.random.uniform(key_list[4], (NI, NX, NT), jnp.float32, -1.5, 1.5) * levels(key_list[4], (NI, NX, NT), ((0, 16), (1, 2)), -0.4, 0.0), -1.5, 1.5)
    weights = jnp.clip(0.2 + 0.8 * jax.random.uniform(key_list[5], (NI, NX, NT), jnp.float32) ** levels(key_list[5], (NI, NX, NT), ((0, 16), (1, 2)), -0.2, 0.2), 0.2, 1.0)
    return {"solution": solution, "residual": residual, "direction": direction, "slope_il": slope_il, "slope_xl": slope_xl, "weights": weights}


damping = 0.3


def time_diff(field):
    padded = jnp.pad(field, ((0, 0), (0, 0), (1, 1)))
    return 0.5 * (padded[:, :, 2:] - padded[:, :, :-2])


def normal_apply(direction, slope_il, slope_xl, weights):
    squared = weights * weights
    keep_il = jnp.arange(direction.shape[0])[:, None, None] < direction.shape[0] - 1
    keep_xl = jnp.arange(direction.shape[1])[None, :, None] < direction.shape[1] - 1
    ahead_il = jnp.concatenate([direction[1:], jnp.zeros_like(direction[:1])], 0)
    ahead_xl = jnp.concatenate([direction[:, 1:], jnp.zeros_like(direction[:, :1])], 1)
    slope_t = time_diff(direction)
    flux_il = jnp.where(keep_il, squared * (ahead_il - direction - slope_il * slope_t), 0.0)
    flux_xl = jnp.where(keep_xl, squared * (ahead_xl - direction - slope_xl * slope_t), 0.0)
    behind_il = jnp.concatenate([jnp.zeros_like(flux_il[:1]), flux_il[:-1]], 0)
    behind_xl = jnp.concatenate([jnp.zeros_like(flux_xl[:, :1]), flux_xl[:, :-1]], 1)
    term_il = behind_il - flux_il + time_diff(slope_il * flux_il)
    term_xl = behind_xl - flux_xl + time_diff(slope_xl * flux_xl)
    return term_il + term_xl + damping * direction


def reference(solution, residual, direction, slope_il, slope_xl, weights):
    image = normal_apply(direction, slope_il, slope_xl, weights)
    norm_old = jnp.sum(residual * residual)
    alpha = norm_old / jnp.sum(direction * image)
    new_solution = solution + alpha * direction
    new_residual = residual - alpha * image
    norm_new = jnp.sum(new_residual * new_residual)
    new_direction = new_residual + (norm_new / norm_old) * direction
    return new_solution, new_residual, new_direction
```

```python
import jax
import jax.numpy as jnp
from jax import lax
from jax.experimental import pallas as pl
from jax.experimental.pallas import tpu as pltpu
from jax.sharding import PartitionSpec as P

damping = 0.3
VMEM_LIMIT = 24 * 1024 * 1024


def swap_pairs(sizes, axis, parity):
    n_il, n_xl = sizes
    size, other = (n_il, n_xl) if axis == 0 else (n_xl, n_il)
    pairs, real = [], False
    for a in range(size):
        mate = a + 1 if a % 2 == parity else a - 1
        inside = 0 <= mate < size
        real = real or inside
        for b in range(other):
            if inside:
                a_to, b_to = mate, b
            else:
                a_to, b_to = a, (b ^ 1 if (b ^ 1) < other else b)
            here, there = ((a, b), (a_to, b_to)) if axis == 0 else ((b, a), (b_to, a_to))
            pairs.append((here[0] * n_xl + here[1], there[0] * n_xl + there[1]))
    return pairs, real


def time_diff(field):
    steps = field.shape[-1]
    at = lax.broadcasted_iota(jnp.int32, field.shape, field.ndim - 1)
    after = jnp.where(at == steps - 1, 0.0, pltpu.roll(field, steps - 1, field.ndim - 1))
    before = jnp.where(at == 0, 0.0, pltpu.roll(field, 1, field.ndim - 1))
    return 0.5 * (after - before)


def make_pack(rows, cols, steps, xl_parities):
    edge = min(8, cols)

    def kernel(place, u_hbm, sil_hbm, sxl_hbm, w_hbm, *rest):
        bufs = rest[: 2 + len(xl_parities)]
        u_low, s_low, w_low, u_up, u_cl, s_cl, w_cl, u_cu, sems = rest[2 + len(xl_parities):]
        copies = [
            pltpu.make_async_copy(src, dst, sems.at[k])
            for k, (src, dst) in enumerate(
                (
                    (u_hbm.at[rows - 1], u_low),
                    (sil_hbm.at[rows - 1], s_low),
                    (w_hbm.at[rows - 1], w_low),
                    (u_hbm.at[0], u_up),
                    (u_hbm.at[:, pl.ds(cols - edge, edge)], u_cl),
                    (sxl_hbm.at[:, pl.ds(cols - edge, edge)], s_cl),
                    (w_hbm.at[:, pl.ds(cols - edge, edge)], w_cl),
                    (u_hbm.at[:, pl.ds(0, edge)], u_cu),
                )
            )
        ]
        for copy in copies:
            copy.start()
        for copy in copies:
            copy.wait()
        il_odd = place[0] % 2
        xl_odd = place[1] % 2
        for parity in range(2):

            @pl.when(il_odd == parity)
            def _(parity=parity):
                buf = bufs[parity]
                u = u_low[...]
                buf[0] = w_low[...] * w_low[...]
                buf[1] = u + s_low[...] * time_diff(u)
                bufs[1 - parity][0] = u_up[...]

        for parity, buf in zip(xl_parities, bufs[2:]):

            @pl.when(xl_odd == parity)
            def _(buf=buf):
                u = u_cl[:, edge - 1, :]
                w = w_cl[:, edge - 1, :]
                buf[pl.ds(0, rows)] = w * w
                buf[pl.ds(rows, rows)] = u + s_cl[:, edge - 1, :] * time_diff(u)

            @pl.when(xl_odd != parity)
            def _(buf=buf):
                u = u_cu[:, 0, :]
                buf[pl.ds(0, rows)] = u
                buf[pl.ds(rows, rows)] = u

    f32 = jnp.float32
    il_buf = jax.ShapeDtypeStruct((2, cols, steps), f32)
    xl_buf = jax.ShapeDtypeStruct((2 * rows, steps), f32)
    hbm = pl.BlockSpec(memory_space=pltpu.HBM)
    vmem = pl.BlockSpec(memory_space=pltpu.VMEM)
    outs = [il_buf, il_buf] + [xl_buf] * len(xl_parities)
    return pl.pallas_call(
        kernel,
        in_specs=[pl.BlockSpec(memory_space=pltpu.SMEM)] + [hbm] * 4,
        out_specs=[vmem] * len(outs),
        out_shape=outs,
        scratch_shapes=[pltpu.VMEM((cols, steps), f32)] * 4
        + [pltpu.VMEM((rows, edge, steps), f32)] * 4
        + [pltpu.SemaphoreType.DMA((8,))],
        compiler_params=pltpu.CompilerParams(vmem_limit_bytes=VMEM_LIMIT),
        name="pack",
    )


def make_inner(rows, cols, steps):
    def kernel(u_ref, sil_ref, sxl_ref, w_ref, img_ref):
        col = lax.broadcasted_iota(jnp.int32, (cols, steps), 0)
        flux_before = None
        for i in range(rows):
            u = u_ref[i]
            w2 = w_ref[i] * w_ref[i]
            slope_t = time_diff(u)
            s_xl = sxl_ref[i]
            ahead = pltpu.roll(u, cols - 1, 0)
            flux_xl = jnp.where(col == cols - 1, 0.0, w2 * (ahead - u - s_xl * slope_t))
            behind = jnp.where(col == 0, 0.0, pltpu.roll(flux_xl, 1, 0))
            image = behind - flux_xl + damping * u
            along = s_xl * flux_xl
            if flux_before is not None:
                image = image + flux_before
            if i < rows - 1:
                s_il = sil_ref[i]
                flux_il = w2 * (u_ref[i + 1] - u - s_il * slope_t)
                image = image - flux_il
                along = along + s_il * flux_il
                flux_before = flux_il
            img_ref[i] = image + time_diff(along)

    vmem = pl.BlockSpec(memory_space=pltpu.VMEM)
    return pl.pallas_call(
        kernel,
        in_specs=[vmem] * 4,
        out_specs=vmem,
        out_shape=jax.ShapeDtypeStruct((rows, cols, steps), jnp.float32),
        compiler_params=pltpu.CompilerParams(vmem_limit_bytes=VMEM_LIMIT),
        name="inner",
    )


def make_edges(rows, cols, steps, n_il, n_xl, xl_parities, n_dev):
    def kernel(place, u_ref, r_ref, sil_ref, sxl_ref, w_ref, part_ref, *rest):
        got = rest[: 2 + len(xl_parities)]
        img_ref, out_ref = rest[2 + len(xl_parities):]
        il, xl = place[0], place[1]
        img_ref[...] = part_ref[...]

        for parity in range(2):
            @pl.when(il % 2 == parity)
            def _(parity=parity):
                @pl.when(il < n_il - 1)
                def _():
                    u, w, s = u_ref[rows - 1], w_ref[rows - 1], sil_ref[rows - 1]
                    flux = w * w * (got[parity][0] - (u + s * time_diff(u)))
                    img_ref[rows - 1] += time_diff(s * flux) - flux

                @pl.when(il > 0)
                def _():
                    other = got[1 - parity]
                    img_ref[0] += other[0] * (u_ref[0] - other[1])

        for parity, buf in zip(xl_parities, got[2:]):

            @pl.when((xl % 2 == parity) & (xl < n_xl - 1))
            def _(buf=buf):
                u, w, s = (ref[:, cols - 1, :] for ref in (u_ref, w_ref, sxl_ref))
                flux = w * w * (buf[pl.ds(0, rows)] - (u + s * time_diff(u)))
                add = time_diff(s * flux) - flux
                for i in range(rows):
                    img_ref[i, pl.ds(cols - 1, 1), :] += add[i : i + 1]

            @pl.when((xl % 2 != parity) & (xl > 0))
            def _(buf=buf):
                add = buf[pl.ds(0, rows)] * (u_ref[:, 0, :] - buf[pl.ds(rows, rows)])
                for i in range(rows):
                    img_ref[i, pl.ds(0, 1), :] += add[i : i + 1]

        zero = jnp.zeros((8, steps), jnp.float32)
        sums = [zero] * 4
        for i in range(rows):
            for j in range(0, cols, 8):
                at = (i, pl.ds(j, 8))
                u, r, image = u_ref[at], r_ref[at], img_ref[at]
                for k, (a, b) in enumerate(((r, r), (u, image), (r, image), (image, image))):
                    sums[k] = sums[k] + a * b
        lane = lax.broadcasted_iota(jnp.int32, (n_dev, 128), 1)
        row = jnp.zeros((n_dev, 128), jnp.float32)
        for k in range(4):
            row = jnp.where(lane == k, jnp.sum(sums[k]), row)
        out_ref[...] = row

    vmem = pl.BlockSpec(memory_space=pltpu.VMEM)
    f32 = jnp.float32
    return pl.pallas_call(
        kernel,
        in_specs=[pl.BlockSpec(memory_space=pltpu.SMEM)] + [vmem] * (8 + len(xl_parities)),
        out_specs=[vmem, vmem],
        out_shape=[
            jax.ShapeDtypeStruct((rows, cols, steps), f32),
            jax.ShapeDtypeStruct((n_dev, 128), f32),
        ],
        compiler_params=pltpu.CompilerParams(vmem_limit_bytes=VMEM_LIMIT),
        name="edges",
    )


def make_update(rows, cols, steps, n_dev):
    def kernel(sums_ref, x_ref, r_ref, u_ref, img_ref, x_hbm, r_hbm, d_hbm, x_out, r_out, d_out, sems):
        total = jnp.sum(sums_ref[...], axis=0, keepdims=True)
        lane = lax.broadcasted_iota(jnp.int32, total.shape, 1)
        norm_old, along, cross, square = (
            jnp.sum(jnp.where(lane == k, total, 0.0), axis=1, keepdims=True) for k in range(4)
        )
        alpha = norm_old / along
        norm_new = norm_old - 2.0 * alpha * cross + alpha * alpha * square
        beta = norm_new / norm_old
        copies = []
        for i in range(rows):
            u = u_ref[i]
            residual = r_ref[i] - alpha * img_ref[i]
            x_out[i] = x_ref[i] + alpha * u
            r_out[i] = residual
            d_out[i] = residual + beta * u
            for k, (src, dst) in enumerate(((x_out, x_hbm), (r_out, r_hbm), (d_out, d_hbm))):
                copy = pltpu.make_async_copy(src.at[i], dst.at[i], sems.at[k, i])
                copy.start()
                copies.append(copy)
        for copy in copies:
            copy.wait()

    vmem = pl.BlockSpec(memory_space=pltpu.VMEM)
    hbm = pl.BlockSpec(memory_space=pltpu.HBM)
    block = jax.ShapeDtypeStruct((rows, cols, steps), jnp.float32)
    return pl.pallas_call(
        kernel,
        in_specs=[vmem] * 5,
        out_specs=[hbm] * 3,
        out_shape=[block] * 3,
        scratch_shapes=[pltpu.VMEM((rows, cols, steps), jnp.float32)] * 3
        + [pltpu.SemaphoreType.DMA((3, rows))],
        compiler_params=pltpu.CompilerParams(vmem_limit_bytes=VMEM_LIMIT),
        name="update",
    )


def solution(mesh):
    n_il, n_xl = mesh.shape["il"], mesh.shape["xl"]
    n_dev = n_il * n_xl
    axes = ("il", "xl")
    il_swaps = [swap_pairs((n_il, n_xl), 0, parity)[0] for parity in range(2)]
    xl_swaps = [swap_pairs((n_il, n_xl), 1, parity) for parity in range(2)]
    xl_parities = [parity for parity in range(2) if xl_swaps[parity][1]]
    swaps = il_swaps + [xl_swaps[parity][0] for parity in xl_parities]

    def body(x, r, u, s_il, s_xl, w):
        rows, cols, steps = u.shape
        place = jnp.stack([lax.axis_index("il"), lax.axis_index("xl")]).astype(jnp.int32)
        stay = [pltpu.with_memory_space_constraint(a, pltpu.HBM) for a in (u, s_il, s_xl, w)]
        sent = make_pack(rows, cols, steps, xl_parities)(place, *stay)
        got = [lax.ppermute(buf, axes, pairs) for buf, pairs in zip(sent, swaps)]
        part = make_inner(rows, cols, steps)(u, s_il, s_xl, w)
        image, row = make_edges(rows, cols, steps, n_il, n_xl, xl_parities, n_dev)(
            place, u, r, s_il, s_xl, w, part, *got
        )
        rows_all = lax.all_to_all(row, axes, 0, 0, tiled=True)
        return make_update(rows, cols, steps, n_dev)(rows_all, x, r, u, image)

    placed = P("il", "xl", None)
    return jax.shard_map(
        body, mesh=mesh, in_specs=(placed,) * 6, out_specs=(placed,) * 3, check_vma=False
    )
```

```python
import jax
import jax.numpy as jnp
from jax import lax
from jax.experimental import pallas as pl
from jax.experimental.pallas import tpu as pltpu
from jax.sharding import PartitionSpec as P


damping = 0.3
VMEM_LIMIT = 16 * 1024 * 1024


def swap_pairs(sizes, axis, parity):
    n_il, n_xl = sizes
    size, other = (n_il, n_xl) if axis == 0 else (n_xl, n_il)
    pairs, real = [], False
    for a in range(size):
        mate = a + 1 if a % 2 == parity else a - 1
        inside = 0 <= mate < size
        real = real or inside
        for b in range(other):
            if inside:
                a_to, b_to = mate, b
            else:
                a_to, b_to = a, (b ^ 1 if (b ^ 1) < other else b)
            here, there = ((a, b), (a_to, b_to)) if axis == 0 else ((b, a), (b_to, a_to))
            pairs.append((here[0] * n_xl + here[1], there[0] * n_xl + there[1]))
    return pairs, real


def time_diff(field):
    steps = field.shape[-1]
    at = lax.broadcasted_iota(jnp.int32, field.shape, field.ndim - 1)
    after = jnp.where(at == steps - 1, 0.0, pltpu.roll(field, steps - 1, field.ndim - 1))
    before = jnp.where(at == 0, 0.0, pltpu.roll(field, 1, field.ndim - 1))
    return 0.5 * (after - before)


def params():
    return pltpu.CompilerParams(vmem_limit_bytes=VMEM_LIMIT)


VMEM = pl.BlockSpec(memory_space=pltpu.VMEM)
HBM = pl.BlockSpec(memory_space=pltpu.HBM)


def f32(*shape):
    return jax.ShapeDtypeStruct(shape, jnp.float32)


def make_pick(rows, cols, steps):
    def kernel(u_hbm, w_hbm, out_ref, sem):
        low = lax.axis_index("il") % 2 == 1

        @pl.when(low)
        def _():
            copy = pltpu.make_async_copy(w_hbm.at[rows - 1], out_ref, sem)
            copy.start()
            copy.wait()

        @pl.when(jnp.logical_not(low))
        def _():
            copy = pltpu.make_async_copy(u_hbm.at[0], out_ref, sem)
            copy.start()
            copy.wait()

    return pl.pallas_call(
        kernel,
        in_specs=[HBM, HBM],
        out_specs=VMEM,
        out_shape=f32(cols, steps),
        scratch_shapes=[pltpu.SemaphoreType.DMA],
        compiler_params=params(),
        name="pick",
    )


def make_pack(rows, cols, steps, xl_parities):
    edge = min(8, cols)

    def kernel(_, u_hbm, sil_hbm, sxl_hbm, w_hbm, g_ref, even_ref, *rest):
        bufs = rest[: len(xl_parities)]
        u_low, s_low, u_cl, s_cl, w_cl, u_cu, sems = rest[len(xl_parities) :]
        il_odd = lax.axis_index("il") % 2
        xl_odd = lax.axis_index("xl") % 2
        last, first = pl.ds(cols - edge, edge), pl.ds(0, edge)
        copies = [
            pltpu.make_async_copy(src, dst, sems.at[k])
            for k, (src, dst) in enumerate(
                (
                    (u_hbm.at[rows - 1], u_low),
                    (sil_hbm.at[rows - 1], s_low),
                    (u_hbm.at[:, last], u_cl),
                    (sxl_hbm.at[:, last], s_cl),
                    (w_hbm.at[:, last], w_cl),
                    (u_hbm.at[:, first], u_cu),
                )
            )
        ]
        for copy in copies:
            copy.start()
        own = [(0, w_hbm.at[rows - 1]), (1, u_hbm.at[0])]
        for parity, src in own:

            @pl.when(il_odd == parity)
            def _(src=src):
                pltpu.make_async_copy(src, even_ref, sems.at[6]).start()

        for copy in copies[:2]:
            copy.wait()
        u = u_low[...]
        g = u + s_low[...] * time_diff(u)
        g_ref[...] = g
        for copy in copies[2:]:
            copy.wait()
        u = u_cl[:, edge - 1, :]
        g = u + s_cl[:, edge - 1, :] * time_diff(u)
        for parity, buf in zip(xl_parities, bufs):
            buf[pl.ds(rows, rows)] = g

            @pl.when(xl_odd == parity)
            def _(buf=buf):
                buf[pl.ds(0, rows)] = w_cl[:, edge - 1, :]

            @pl.when(xl_odd != parity)
            def _(buf=buf):
                buf[pl.ds(0, rows)] = u_cu[:, 0, :]

        for parity, src in own:

            @pl.when(il_odd == parity)
            def _(src=src):
                pltpu.make_async_copy(src, even_ref, sems.at[6]).wait()

    outs = [f32(cols, steps), f32(cols, steps)] + [f32(2 * rows, steps)] * len(xl_parities)
    return pl.pallas_call(
        kernel,
        in_specs=[pl.BlockSpec(memory_space=pl.ANY)] + [HBM] * 4,
        out_specs=[VMEM] * len(outs),
        out_shape=outs,
        scratch_shapes=[pltpu.VMEM((cols, steps), jnp.float32)] * 2
        + [pltpu.VMEM((rows, edge, steps), jnp.float32)] * 4
        + [pltpu.SemaphoreType.DMA((7,))],
        compiler_params=params(),
        name="pack",
    )


def add_products(sums, u, r, image):
    return [s + a * b for s, (a, b) in zip(sums, ((u, image), (r, image), (image, image)))]


def make_inner(rows, cols, steps):
    def kernel(u_ref, r_ref, sil_ref, sxl_ref, w_ref, img_ref, sums_ref):
        col = lax.broadcasted_iota(jnp.int32, (cols, steps), 0)
        flux_before = None
        norm = jnp.zeros((8, steps), jnp.float32)
        sums = [norm] * 3
        for i in range(rows):
            u = u_ref[i]
            w2 = w_ref[i] * w_ref[i]
            slope_t = time_diff(u)
            s_xl = sxl_ref[i]
            ahead = pltpu.roll(u, cols - 1, 0)
            flux_xl = jnp.where(col == cols - 1, 0.0, w2 * (ahead - u - s_xl * slope_t))
            behind = jnp.where(col == 0, 0.0, pltpu.roll(flux_xl, 1, 0))
            image = behind - flux_xl + damping * u
            along = s_xl * flux_xl
            if flux_before is not None:
                image = image + flux_before
            if i < rows - 1:
                s_il = sil_ref[i]
                flux_il = w2 * (u_ref[i + 1] - u - s_il * slope_t)
                image = image - flux_il
                along = along + s_il * flux_il
                flux_before = flux_il
            img_ref[i] = image + time_diff(along)
            for j in range(0, cols, 8):
                at = (i, pl.ds(j, 8))
                r = r_ref[at]
                norm = norm + r * r
                if 0 < i < rows - 1 and 0 < j < cols - 8:
                    sums = add_products(sums, u_ref[at], r, img_ref[at])
        for k, value in enumerate([norm] + sums):
            sums_ref[k] = value

    return pl.pallas_call(
        kernel,
        in_specs=[VMEM] * 5,
        out_specs=[VMEM] * 2,
        out_shape=[f32(rows, cols, steps), f32(4, 8, steps)],
        compiler_params=params(),
        name="inner",
    )


def make_edges(rows, cols, steps, n_il, n_xl, xl_parities, n_dev):
    def kernel(u_ref, r_ref, sil_ref, sxl_ref, w_ref, part_ref, sums_ref, mine_ref, even_ref, odd_ref, g_ref, *rest):
        bufs = rest[:-2]
        img_ref, out_ref = rest[-2:]
        il, xl = lax.axis_index("il"), lax.axis_index("xl")

        def low(ahead):
            w = w_ref[rows - 1]
            flux = w * w * (ahead - mine_ref[...])
            img_ref[rows - 1] = part_ref[rows - 1] + (time_diff(sil_ref[rows - 1] * flux) - flux)

        def high(w, g):
            img_ref[0] += w * w * (u_ref[0] - g)

        for i in range(rows):
            img_ref[i] = part_ref[i]

        @pl.when((il % 2 == 0) & (il < n_il - 1))
        def _():
            low(even_ref[...])

        @pl.when((il % 2 == 1) & (il < n_il - 1))
        def _():
            low(odd_ref[...])

        @pl.when((il % 2 == 0) & (il > 0))
        def _():
            high(odd_ref[...], g_ref[...])

        @pl.when(il % 2 == 1)
        def _():
            high(even_ref[...], g_ref[...])

        half = len(xl_parities)
        for parity, mine, got in zip(xl_parities, bufs[:half], bufs[half:]):

            @pl.when((xl % 2 == parity) & (xl < n_xl - 1))
            def _(mine=mine, got=got):
                w = mine[pl.ds(0, rows)]
                flux = w * w * (got[pl.ds(0, rows)] - mine[pl.ds(rows, rows)])
                add = time_diff(sxl_ref[:, cols - 1, :] * flux) - flux
                for i in range(rows):
                    img_ref[i, pl.ds(cols - 1, 1), :] += add[i : i + 1]

            @pl.when((xl % 2 != parity) & (xl > 0))
            def _(got=got):
                w = got[pl.ds(0, rows)]
                add = w * w * (u_ref[:, 0, :] - got[pl.ds(rows, rows)])
                for i in range(rows):
                    img_ref[i, pl.ds(0, 1), :] += add[i : i + 1]

        sums = [sums_ref[k] for k in range(1, 4)]
        for i in range(rows):
            for j in range(0, cols, 8):
                if not (0 < i < rows - 1 and 0 < j < cols - 8):
                    at = (i, pl.ds(j, 8))
                    sums = add_products(sums, u_ref[at], r_ref[at], img_ref[at])
        lane = lax.broadcasted_iota(jnp.int32, (1, 128), 1)
        row = jnp.zeros((1, 128), jnp.float32)
        for k, value in enumerate([sums_ref[0]] + sums):
            value = sum(value[:, j : j + 128] for j in range(128, steps, 128)) + value[:, :128]
            value = jnp.sum(jnp.sum(value, axis=0, keepdims=True), axis=1, keepdims=True)
            row = jnp.where(lane == k, value, row)
        out_ref[...] = jnp.broadcast_to(row, (n_dev, 128))

    return pl.pallas_call(
        kernel,
        in_specs=[VMEM] * (11 + 2 * len(xl_parities)),
        out_specs=[VMEM, VMEM],
        out_shape=[f32(rows, cols, steps), f32(n_dev, 128)],
        input_output_aliases={5: 0},
        compiler_params=params(),
        name="edges",
    )


def make_update(rows, cols, steps):
    def kernel(sums_ref, x_ref, r_ref, u_ref, img_ref, x_hbm, r_hbm, d_hbm, x_out, r_out, d_out, sems):
        total = jnp.sum(sums_ref[...], axis=0, keepdims=True)
        lane = lax.broadcasted_iota(jnp.int32, total.shape, 1)
        norm_old, along, cross, square = (
            jnp.sum(jnp.where(lane == k, total, 0.0), axis=1, keepdims=True) for k in range(4)
        )
        alpha = norm_old / along
        norm_new = norm_old - 2.0 * alpha * cross + alpha * alpha * square
        beta = norm_new / norm_old
        copies = []
        for i in range(rows):
            u = u_ref[i]
            residual = r_ref[i] - alpha * img_ref[i]
            x_out[i] = x_ref[i] + alpha * u
            r_out[i] = residual
            d_out[i] = residual + beta * u
            for k, (src, dst) in enumerate(((x_out, x_hbm), (r_out, r_hbm), (d_out, d_hbm))):
                copy = pltpu.make_async_copy(src.at[i], dst.at[i], sems.at[k, i])
                copy.start()
                copies.append(copy)
        for copy in copies:
            copy.wait()

    return pl.pallas_call(
        kernel,
        in_specs=[VMEM] * 5,
        out_specs=[HBM] * 3,
        out_shape=[f32(rows, cols, steps)] * 3,
        scratch_shapes=[pltpu.VMEM((rows, cols, steps), jnp.float32)] * 3
        + [pltpu.SemaphoreType.DMA((3, rows))],
        compiler_params=params(),
        name="update",
    )


def solution(mesh):
    n_il, n_xl = mesh.shape["il"], mesh.shape["xl"]
    n_dev = n_il * n_xl
    axes = ("il", "xl")
    even_swap, odd_swap = (swap_pairs((n_il, n_xl), 0, parity)[0] for parity in range(2))
    up = [(i, (i + 1) % n_il) for i in range(n_il)]
    xl_swaps = [swap_pairs((n_il, n_xl), 1, parity) for parity in range(2)]
    xl_parities = [parity for parity in range(2) if xl_swaps[parity][1]]

    def step(x, r, u, s_il, s_xl, w):
        rows, cols, steps = u.shape
        stay = [pltpu.with_memory_space_constraint(a, pltpu.HBM) for a in (u, s_il, s_xl, w)]
        picked = make_pick(rows, cols, steps)(stay[0], stay[3])
        odd = lax.ppermute(picked, axes, odd_swap)
        g, first, *xl_sent = make_pack(rows, cols, steps, xl_parities)(picked, *stay)
        g_got = lax.ppermute(g, "il", up)
        xl_got = []
        for p, buf in zip(xl_parities, xl_sent):
            xl_got.append(lax.ppermute(buf, axes, xl_swaps[p][0]))
        even = lax.ppermute(first, axes, even_swap)
        part, sums = make_inner(rows, cols, steps)(u, r, s_il, s_xl, w)
        image, row = make_edges(rows, cols, steps, n_il, n_xl, xl_parities, n_dev)(
            u, r, s_il, s_xl, w, part, sums, g, even, odd, g_got, *xl_sent, *xl_got
        )
        rows_all = lax.all_to_all(row, axes, 0, 0, tiled=True)
        return make_update(rows, cols, steps)(rows_all, x, r, u, image)

    placed = P("il", "xl", None)
    return jax.shard_map(step, mesh=mesh, in_specs=(placed,) * 6, out_specs=(placed,) * 3, check_vma=False)
```

```python
import jax
import jax.numpy as jnp
from jax import lax
from jax.experimental import pallas as pl
from jax.experimental.pallas import tpu as pltpu
from jax.sharding import PartitionSpec as P


damping = 0.3
VMEM_LIMIT = 16 * 1024 * 1024


def swap_pairs(sizes, axis, parity):
    n_il, n_xl = sizes
    size, other = (n_il, n_xl) if axis == 0 else (n_xl, n_il)
    pairs, real = [], False
    for a in range(size):
        mate = a + 1 if a % 2 == parity else a - 1
        inside = 0 <= mate < size
        real = real or inside
        for b in range(other):
            if inside:
                a_to, b_to = mate, b
            else:
                a_to, b_to = a, (b ^ 1 if (b ^ 1) < other else b)
            here, there = ((a, b), (a_to, b_to)) if axis == 0 else ((b, a), (b_to, a_to))
            pairs.append((here[0] * n_xl + here[1], there[0] * n_xl + there[1]))
    return pairs, real


def time_diff(field):
    steps = field.shape[-1]
    at = lax.broadcasted_iota(jnp.int32, field.shape, field.ndim - 1)
    after = jnp.where(at == steps - 1, 0.0, pltpu.roll(field, steps - 1, field.ndim - 1))
    before = jnp.where(at == 0, 0.0, pltpu.roll(field, 1, field.ndim - 1))
    return 0.5 * (after - before)


def params():
    return pltpu.CompilerParams(vmem_limit_bytes=VMEM_LIMIT)


VMEM = pl.BlockSpec(memory_space=pltpu.VMEM)
HBM = pl.BlockSpec(memory_space=pltpu.HBM)


def f32(*shape):
    return jax.ShapeDtypeStruct(shape, jnp.float32)


def make_slope_row(rows, cols, steps):
    def kernel(u_hbm, sil_hbm, g_ref, u_ref, s_ref, sems):
        @pl.when(lax.axis_index("il") % 2 == 1)
        def _():
            pairs = ((u_hbm.at[rows - 1], u_ref), (sil_hbm.at[rows - 1], s_ref))
            copies = [pltpu.make_async_copy(src, dst, sems.at[k]) for k, (src, dst) in enumerate(pairs)]
            for copy in copies:
                copy.start()
            for copy in copies:
                copy.wait()
            u = u_ref[...]
            g_ref[...] = u + s_ref[...] * time_diff(u)

    return pl.pallas_call(
        kernel,
        in_specs=[HBM] * 2,
        out_specs=VMEM,
        out_shape=f32(cols, steps),
        scratch_shapes=[pltpu.VMEM((cols, steps), jnp.float32)] * 2 + [pltpu.SemaphoreType.DMA((2,))],
        compiler_params=params(),
        name="slope_row",
    )


def make_pick(rows, cols, steps):
    def kernel(_, u_ref, w_ref, odd_ref):
        il_odd = lax.axis_index("il") % 2

        @pl.when(il_odd == 0)
        def _():
            odd_ref[...] = u_ref[0]

        @pl.when(il_odd == 1)
        def _():
            odd_ref[...] = w_ref[rows - 1]

    return pl.pallas_call(
        kernel,
        in_specs=[pl.BlockSpec(memory_space=pl.ANY), VMEM, VMEM],
        out_specs=VMEM,
        out_shape=f32(cols, steps),
        compiler_params=params(),
        name="pick",
    )


def make_pack(rows, cols, steps, xl_parities):
    edge = min(8, cols)

    def kernel(_, u_hbm, sil_hbm, sxl_hbm, w_hbm, even_ref, *rest):
        bufs = rest[: len(xl_parities)]
        u_low, s_low, u_cl, s_cl, w_cl, u_cu, sems = rest[len(xl_parities) :]
        il_odd = lax.axis_index("il") % 2
        xl_odd = lax.axis_index("xl") % 2
        last, first = pl.ds(cols - edge, edge), pl.ds(0, edge)
        pairs = (
            (u_hbm.at[:, last], u_cl),
            (sxl_hbm.at[:, last], s_cl),
            (w_hbm.at[:, last], w_cl),
            (u_hbm.at[:, first], u_cu),
        )
        copies = [pltpu.make_async_copy(src, dst, sems.at[k]) for k, (src, dst) in enumerate(pairs)]
        for copy in copies:
            copy.start()

        @pl.when(il_odd == 0)
        def _():
            pairs = ((u_hbm.at[rows - 1], u_low), (sil_hbm.at[rows - 1], s_low), (w_hbm.at[rows - 1], even_ref.at[0]))
            low = [pltpu.make_async_copy(src, dst, sems.at[4 + k]) for k, (src, dst) in enumerate(pairs)]
            for copy in low:
                copy.start()
            for copy in low:
                copy.wait()
            u = u_low[...]
            even_ref[1] = u + s_low[...] * time_diff(u)

        @pl.when(il_odd == 1)
        def _():
            copy = pltpu.make_async_copy(u_hbm.at[0], even_ref.at[0], sems.at[4])
            copy.start()
            copy.wait()

        for copy in copies:
            copy.wait()
        u = u_cl[:, edge - 1, :]
        g = u + s_cl[:, edge - 1, :] * time_diff(u)
        for parity, buf in zip(xl_parities, bufs):
            buf[pl.ds(rows, rows)] = g

            @pl.when(xl_odd == parity)
            def _(buf=buf):
                buf[pl.ds(0, rows)] = w_cl[:, edge - 1, :]

            @pl.when(xl_odd != parity)
            def _(buf=buf):
                buf[pl.ds(0, rows)] = u_cu[:, 0, :]

    outs = [f32(2, cols, steps)] + [f32(2 * rows, steps)] * len(xl_parities)
    return pl.pallas_call(
        kernel,
        in_specs=[pl.BlockSpec(memory_space=pl.ANY)] + [HBM] * 4,
        out_specs=[VMEM] * len(outs),
        out_shape=outs,
        scratch_shapes=[pltpu.VMEM((cols, steps), jnp.float32)] * 2
        + [pltpu.VMEM((rows, edge, steps), jnp.float32)] * 4
        + [pltpu.SemaphoreType.DMA((7,))],
        compiler_params=params(),
        name="pack",
    )


def edge_tiles(cols):
    return sorted({0, cols - 8})


def inner_tiles(cols):
    return range(8, cols - 8, 8)


def add_products(sums, tiles, u_ref, r_ref, img_ref):
    for i, j in tiles:
        at = (i, pl.ds(j, 8))
        u, r, image = u_ref[at], r_ref[at], img_ref[at]
        sums = [s + a * b for s, (a, b) in zip(sums, ((u, image), (r, image), (image, image)))]
    return sums


def lower_flux(w, ahead, g, slope):
    flux = w * w * (ahead - g)
    return time_diff(slope * flux) - flux


def make_inner(rows, cols, steps):
    def kernel(u_ref, r_ref, sil_ref, sxl_ref, w_ref, img_ref, sums_ref):
        col = lax.broadcasted_iota(jnp.int32, (cols, steps), 0)
        flux_before = None
        norm = jnp.zeros((8, steps), jnp.float32)
        sums = [norm] * 3
        for i in range(rows):
            u = u_ref[i]
            w2 = w_ref[i] * w_ref[i]
            slope_t = time_diff(u)
            s_xl = sxl_ref[i]
            ahead = pltpu.roll(u, cols - 1, 0)
            flux_xl = jnp.where(col == cols - 1, 0.0, w2 * (ahead - u - s_xl * slope_t))
            behind = jnp.where(col == 0, 0.0, pltpu.roll(flux_xl, 1, 0))
            image = behind - flux_xl + damping * u
            along = s_xl * flux_xl
            if flux_before is not None:
                image = image + flux_before
            if i < rows - 1:
                s_il = sil_ref[i]
                flux_il = w2 * (u_ref[i + 1] - u - s_il * slope_t)
                image = image - flux_il
                along = along + s_il * flux_il
                flux_before = flux_il
            img_ref[i] = image + time_diff(along)
            for j in range(0, cols, 8):
                r = r_ref[i, pl.ds(j, 8)]
                norm = norm + r * r
            if 0 < i < rows - 1:
                sums = add_products(sums, [(i, j) for j in inner_tiles(cols)], u_ref, r_ref, img_ref)
        for k, value in enumerate([norm] + sums):
            sums_ref[k] = value

    return pl.pallas_call(
        kernel,
        in_specs=[VMEM] * 5,
        out_specs=[VMEM] * 2,
        out_shape=[f32(rows, cols, steps), f32(4, 8, steps)],
        compiler_params=params(),
        name="inner",
    )


def make_even_edge(rows, cols, steps, n_il):
    def kernel(u_ref, r_ref, sil_ref, w_ref, mine_ref, got_ref, _, img_in, sums_in, img_ref, sums_ref):
        il = lax.axis_index("il")

        def add(row):
            if rows > 1:
                sums = add_products(
                    [sums_ref[k] for k in range(1, 4)], [(row, j) for j in inner_tiles(cols)], u_ref, r_ref, img_ref
                )
                for k, value in enumerate(sums):
                    sums_ref[k + 1] = value

        @pl.when(il % 2 == 0)
        def _():
            @pl.when(il < n_il - 1)
            def _():
                img_ref[rows - 1] += lower_flux(w_ref[rows - 1], got_ref[0], mine_ref[1], sil_ref[rows - 1])

            add(rows - 1)

        @pl.when(il % 2 == 1)
        def _():
            img_ref[0] += got_ref[0] * got_ref[0] * (u_ref[0] - got_ref[1])
            add(0)

    return pl.pallas_call(
        kernel,
        in_specs=[VMEM] * 6 + [pl.BlockSpec(memory_space=pl.ANY)] + [VMEM] * 2,
        out_specs=[VMEM] * 2,
        out_shape=[f32(rows, cols, steps), f32(4, 8, steps)],
        input_output_aliases={7: 0, 8: 1},
        compiler_params=params(),
        name="even_edge",
    )


def make_edges(rows, cols, steps, n_il, n_xl, xl_parities, n_dev):
    def kernel(u_ref, r_ref, sil_ref, sxl_ref, w_ref, part_ref, sums_in, own_ref, odd_ref, g_ref, *rest):
        bufs = rest[:-3]
        img_ref, out_ref, sums_ref = rest[-3:]
        il, xl = lax.axis_index("il"), lax.axis_index("xl")

        half = len(xl_parities)
        for parity, mine, got in zip(xl_parities, bufs[:half], bufs[half:]):

            @pl.when((xl % 2 == parity) & (xl < n_xl - 1))
            def _(mine=mine, got=got):
                here, there = pl.ds(0, rows), pl.ds(rows, rows)
                add = lower_flux(mine[here], got[here], mine[there], sxl_ref[:, cols - 1, :])
                for i in range(rows):
                    img_ref[i, pl.ds(cols - 1, 1), :] += add[i : i + 1]

            @pl.when((xl % 2 != parity) & (xl > 0))
            def _(got=got):
                w = got[pl.ds(0, rows)]
                add = w * w * (u_ref[:, 0, :] - got[pl.ds(rows, rows)])
                for i in range(rows):
                    img_ref[i, pl.ds(0, 1), :] += add[i : i + 1]

        def add(row):
            tiles = [(row, j) for j in inner_tiles(cols)]
            tiles += [(i, j) for i in range(rows) for j in edge_tiles(cols)]
            sums = add_products([sums_in[k] for k in range(1, 4)], tiles, u_ref, r_ref, img_ref)
            for k, value in enumerate(sums):
                sums_ref[k] = value

        @pl.when(il % 2 == 0)
        def _():
            @pl.when(il > 0)
            def _():
                w = odd_ref[...]
                img_ref[0] += w * w * (u_ref[0] - g_ref[...])

            add(0)

        @pl.when(il % 2 == 1)
        def _():
            @pl.when(il < n_il - 1)
            def _():
                img_ref[rows - 1] += lower_flux(w_ref[rows - 1], odd_ref[...], own_ref[...], sil_ref[rows - 1])

            add(rows - 1)

        lane = lax.broadcasted_iota(jnp.int32, (1, 128), 1)
        row = jnp.zeros((1, 128), jnp.float32)
        for k, value in enumerate([sums_in[0]] + [sums_ref[k] for k in range(3)]):
            value = sum(value[:, j : j + 128] for j in range(128, steps, 128)) + value[:, :128]
            value = jnp.sum(jnp.sum(value, axis=0, keepdims=True), axis=1, keepdims=True)
            row = jnp.where(lane == k, value, row)
        out_ref[...] = jnp.broadcast_to(row, (n_dev, 128))

    return pl.pallas_call(
        kernel,
        in_specs=[VMEM] * (10 + 2 * len(xl_parities)),
        out_specs=[VMEM, VMEM],
        out_shape=[f32(rows, cols, steps), f32(n_dev, 128)],
        input_output_aliases={5: 0},
        scratch_shapes=[pltpu.VMEM((3, 8, steps), jnp.float32)],
        compiler_params=params(),
        name="edges",
    )


def make_update(rows, cols, steps):
    piece = 64 if cols % 64 == 0 else cols

    def kernel(sums_ref, x_ref, r_ref, u_ref, img_ref, x_hbm, r_hbm, d_hbm, x_out, r_out, d_out, sems):
        total = jnp.sum(sums_ref[...], axis=0, keepdims=True)
        lane = lax.broadcasted_iota(jnp.int32, total.shape, 1)
        norm_old, along, cross, square = (
            jnp.sum(jnp.where(lane == k, total, 0.0), axis=1, keepdims=True) for k in range(4)
        )
        alpha = norm_old / along
        norm_new = norm_old - 2.0 * alpha * cross + alpha * alpha * square
        beta = norm_new / norm_old
        copies = []
        pieces = [(i, pl.ds(j, piece)) for i in range(rows) for j in range(0, cols, piece)]
        for n, at in enumerate(pieces):
            u = u_ref[at]
            residual = r_ref[at] - alpha * img_ref[at]
            x_out[at] = x_ref[at] + alpha * u
            r_out[at] = residual
            d_out[at] = residual + beta * u
            for k, (src, dst) in enumerate(((x_out, x_hbm), (r_out, r_hbm), (d_out, d_hbm))):
                copy = pltpu.make_async_copy(src.at[at], dst.at[at], sems.at[k, n])
                copy.start()
                copies.append(copy)
        for copy in copies:
            copy.wait()

    return pl.pallas_call(
        kernel,
        in_specs=[VMEM] * 5,
        out_specs=[HBM] * 3,
        out_shape=[f32(rows, cols, steps)] * 3,
        scratch_shapes=[pltpu.VMEM((rows, cols, steps), jnp.float32)] * 3
        + [pltpu.SemaphoreType.DMA((3, rows * cols // piece))],
        compiler_params=params(),
        name="update",
    )


def solution(mesh):
    n_il, n_xl = mesh.shape["il"], mesh.shape["xl"]
    n_dev = n_il * n_xl
    axes = ("il", "xl")
    even_swap, odd_swap = (swap_pairs((n_il, n_xl), 0, parity)[0] for parity in range(2))
    up = [(i, (i + 1) % n_il) for i in range(n_il)]
    xl_swaps = [swap_pairs((n_il, n_xl), 1, parity) for parity in range(2)]
    xl_parities = [parity for parity in range(2) if xl_swaps[parity][1]]

    def step(x, r, u, s_il, s_xl, w):
        rows, cols, steps = u.shape
        stay = [pltpu.with_memory_space_constraint(a, pltpu.HBM) for a in (u, s_il, s_xl, w)]
        g = make_slope_row(rows, cols, steps)(stay[0], stay[1])
        g_got = lax.ppermute(g, "il", up)
        odd_sent = make_pick(rows, cols, steps)(g, u, w)
        odd = lax.ppermute(odd_sent, axes, odd_swap)
        even_sent, *xl_sent = make_pack(rows, cols, steps, xl_parities)(odd_sent, *stay)
        xl_got = []
        for p, buf in zip(xl_parities, xl_sent):
            xl_got.append(lax.ppermute(buf, axes, xl_swaps[p][0]))
        even = lax.ppermute(even_sent, axes, even_swap)
        part, sums = make_inner(rows, cols, steps)(u, r, s_il, s_xl, w)
        part, sums = make_even_edge(rows, cols, steps, n_il)(u, r, s_il, w, even_sent, even, even_sent, part, sums)
        image, row = make_edges(rows, cols, steps, n_il, n_xl, xl_parities, n_dev)(
            u, r, s_il, s_xl, w, part, sums, g, odd, g_got, *xl_sent, *xl_got
        )
        rows_all = lax.all_to_all(row, axes, 0, 0, tiled=True)
        return make_update(rows, cols, steps)(rows_all, x, r, u, image)

    placed = P("il", "xl", None)
    return jax.shard_map(step, mesh=mesh, in_specs=(placed,) * 6, out_specs=(placed,) * 3, check_vma=False)
```

```python
import jax
import jax.numpy as jnp
from jax import lax
from jax.experimental import pallas as pl
from jax.experimental.pallas import tpu as pltpu
from jax.sharding import PartitionSpec as P


damping = 0.3
VMEM_LIMIT = 16 * 1024 * 1024


def swap_pairs(sizes, axis, parity):
    n_il, n_xl = sizes
    size, other = (n_il, n_xl) if axis == 0 else (n_xl, n_il)
    pairs, real = [], False
    for a in range(size):
        mate = a + 1 if a % 2 == parity else a - 1
        inside = 0 <= mate < size
        real = real or inside
        for b in range(other):
            if inside:
                a_to, b_to = mate, b
            else:
                a_to, b_to = a, (b ^ 1 if (b ^ 1) < other else b)
            here, there = ((a, b), (a_to, b_to)) if axis == 0 else ((b, a), (b_to, a_to))
            pairs.append((here[0] * n_xl + here[1], there[0] * n_xl + there[1]))
    return pairs, real


def time_diff(field):
    steps = field.shape[-1]
    at = lax.broadcasted_iota(jnp.int32, field.shape, field.ndim - 1)
    after = jnp.where(at == steps - 1, 0.0, pltpu.roll(field, steps - 1, field.ndim - 1))
    before = jnp.where(at == 0, 0.0, pltpu.roll(field, 1, field.ndim - 1))
    return 0.5 * (after - before)


def params():
    return pltpu.CompilerParams(vmem_limit_bytes=VMEM_LIMIT)


VMEM = pl.BlockSpec(memory_space=pltpu.VMEM)
HBM = pl.BlockSpec(memory_space=pltpu.HBM)


def f32(*shape):
    return jax.ShapeDtypeStruct(shape, jnp.float32)


def make_slope_row(rows, cols, steps):
    def kernel(u_hbm, sil_hbm, g_ref, u_ref, s_ref, sems):
        @pl.when(lax.axis_index("il") % 2 == 1)
        def _():
            pairs = ((u_hbm.at[rows - 1], u_ref), (sil_hbm.at[rows - 1], s_ref))
            copies = [pltpu.make_async_copy(src, dst, sems.at[k]) for k, (src, dst) in enumerate(pairs)]
            for copy in copies:
                copy.start()
            for copy in copies:
                copy.wait()
            u = u_ref[...]
            g_ref[...] = u + s_ref[...] * time_diff(u)

    return pl.pallas_call(
        kernel,
        in_specs=[HBM] * 2,
        out_specs=VMEM,
        out_shape=f32(cols, steps),
        scratch_shapes=[pltpu.VMEM((cols, steps), jnp.float32)] * 2 + [pltpu.SemaphoreType.DMA((2,))],
        compiler_params=params(),
        name="slope_row",
    )


def make_pick(rows, cols, steps):
    def kernel(_, u_ref, w_ref, odd_ref):
        il_odd = lax.axis_index("il") % 2

        @pl.when(il_odd == 0)
        def _():
            odd_ref[...] = u_ref[0]

        @pl.when(il_odd == 1)
        def _():
            odd_ref[...] = w_ref[rows - 1]

    return pl.pallas_call(
        kernel,
        in_specs=[pl.BlockSpec(memory_space=pl.ANY), VMEM, VMEM],
        out_specs=VMEM,
        out_shape=f32(cols, steps),
        compiler_params=params(),
        name="pick",
    )


def make_pack(rows, cols, steps, xl_parities):
    def kernel(_, u_ref, sxl_ref, w_ref, *bufs):
        xl_odd = lax.axis_index("xl") % 2
        u = u_ref[:, cols - 1, :]
        g = u + sxl_ref[:, cols - 1, :] * time_diff(u)
        for parity, buf in zip(xl_parities, bufs):
            buf[pl.ds(rows, rows)] = g

            @pl.when(xl_odd == parity)
            def _(buf=buf):
                buf[pl.ds(0, rows)] = w_ref[:, cols - 1, :]

            @pl.when(xl_odd != parity)
            def _(buf=buf):
                buf[pl.ds(0, rows)] = u_ref[:, 0, :]

    return pl.pallas_call(
        kernel,
        in_specs=[pl.BlockSpec(memory_space=pl.ANY)] + [VMEM] * 3,
        out_specs=[VMEM] * len(xl_parities),
        out_shape=[f32(2 * rows, steps)] * len(xl_parities),
        compiler_params=params(),
        name="pack",
    )


def make_pair(rows, cols, steps):
    def kernel(_, u_ref, sil_ref, w_ref, even_ref):
        il_odd = lax.axis_index("il") % 2

        @pl.when(il_odd == 0)
        def _():
            u = u_ref[rows - 1]
            even_ref[0] = w_ref[rows - 1]
            even_ref[1] = u + sil_ref[rows - 1] * time_diff(u)

        @pl.when(il_odd == 1)
        def _():
            even_ref[0] = u_ref[0]

    return pl.pallas_call(
        kernel,
        in_specs=[pl.BlockSpec(memory_space=pl.ANY)] + [VMEM] * 3,
        out_specs=VMEM,
        out_shape=f32(2, cols, steps),
        compiler_params=params(),
        name="pair",
    )


def edge_tiles(cols):
    return sorted({0, cols - 8})


def inner_tiles(cols):
    return range(8, cols - 8, 8)


def add_products(sums, tiles, u_ref, r_ref, img_ref):
    for i, j in tiles:
        at = (i, pl.ds(j, 8))
        u, r, image = u_ref[at], r_ref[at], img_ref[at]
        sums = [s + a * b for s, (a, b) in zip(sums, ((u, image), (r, image), (image, image)))]
    return sums


def lower_flux(w, ahead, g, slope):
    flux = w * w * (ahead - g)
    return time_diff(slope * flux) - flux


def make_inner(rows, cols, steps):
    def kernel(u_ref, r_ref, sil_ref, sxl_ref, w_ref, img_ref, sums_ref):
        col = lax.broadcasted_iota(jnp.int32, (cols, steps), 0)
        flux_before = None
        norm = jnp.zeros((8, steps), jnp.float32)
        sums = [norm] * 3
        for i in range(rows):
            u = u_ref[i]
            w2 = w_ref[i] * w_ref[i]
            slope_t = time_diff(u)
            s_xl = sxl_ref[i]
            ahead = pltpu.roll(u, cols - 1, 0)
            flux_xl = jnp.where(col == cols - 1, 0.0, w2 * (ahead - u - s_xl * slope_t))
            behind = jnp.where(col == 0, 0.0, pltpu.roll(flux_xl, 1, 0))
            image = behind - flux_xl + damping * u
            along = s_xl * flux_xl
            if flux_before is not None:
                image = image + flux_before
            if i < rows - 1:
                s_il = sil_ref[i]
                flux_il = w2 * (u_ref[i + 1] - u - s_il * slope_t)
                image = image - flux_il
                along = along + s_il * flux_il
                flux_before = flux_il
            img_ref[i] = image + time_diff(along)
            for j in range(0, cols, 8):
                r = r_ref[i, pl.ds(j, 8)]
                norm = norm + r * r
            if 0 < i < rows - 1:
                sums = add_products(sums, [(i, j) for j in inner_tiles(cols)], u_ref, r_ref, img_ref)
        for k, value in enumerate([norm] + sums):
            sums_ref[k] = value

    return pl.pallas_call(
        kernel,
        in_specs=[VMEM] * 5,
        out_specs=[VMEM] * 2,
        out_shape=[f32(rows, cols, steps), f32(4, 8, steps)],
        compiler_params=params(),
        name="inner",
    )


def make_even_edge(rows, cols, steps, n_il):
    def kernel(u_ref, r_ref, sil_ref, w_ref, mine_ref, got_ref, _, img_in, sums_in, img_ref, sums_ref):
        il = lax.axis_index("il")

        def add(row):
            if rows > 1:
                sums = add_products(
                    [sums_ref[k] for k in range(1, 4)], [(row, j) for j in inner_tiles(cols)], u_ref, r_ref, img_ref
                )
                for k, value in enumerate(sums):
                    sums_ref[k + 1] = value

        @pl.when(il % 2 == 0)
        def _():
            @pl.when(il < n_il - 1)
            def _():
                img_ref[rows - 1] += lower_flux(w_ref[rows - 1], got_ref[0], mine_ref[1], sil_ref[rows - 1])

            add(rows - 1)

        @pl.when(il % 2 == 1)
        def _():
            img_ref[0] += got_ref[0] * got_ref[0] * (u_ref[0] - got_ref[1])
            add(0)

    return pl.pallas_call(
        kernel,
        in_specs=[VMEM] * 6 + [pl.BlockSpec(memory_space=pl.ANY)] + [VMEM] * 2,
        out_specs=[VMEM] * 2,
        out_shape=[f32(rows, cols, steps), f32(4, 8, steps)],
        input_output_aliases={7: 0, 8: 1},
        compiler_params=params(),
        name="even_edge",
    )


def make_edges(rows, cols, steps, n_il, n_xl, xl_parities, n_dev):
    def kernel(u_ref, r_ref, sil_ref, sxl_ref, w_ref, part_ref, sums_in, own_ref, odd_ref, g_ref, *rest):
        bufs = rest[:-3]
        img_ref, out_ref, sums_ref = rest[-3:]
        il, xl = lax.axis_index("il"), lax.axis_index("xl")

        half = len(xl_parities)
        for parity, mine, got in zip(xl_parities, bufs[:half], bufs[half:]):

            @pl.when((xl % 2 == parity) & (xl < n_xl - 1))
            def _(mine=mine, got=got):
                here, there = pl.ds(0, rows), pl.ds(rows, rows)
                add = lower_flux(mine[here], got[here], mine[there], sxl_ref[:, cols - 1, :])
                for i in range(rows):
                    img_ref[i, pl.ds(cols - 1, 1), :] += add[i : i + 1]

            @pl.when((xl % 2 != parity) & (xl > 0))
            def _(got=got):
                w = got[pl.ds(0, rows)]
                add = w * w * (u_ref[:, 0, :] - got[pl.ds(rows, rows)])
                for i in range(rows):
                    img_ref[i, pl.ds(0, 1), :] += add[i : i + 1]

        def add(row):
            tiles = [(row, j) for j in inner_tiles(cols)]
            tiles += [(i, j) for i in range(rows) for j in edge_tiles(cols)]
            sums = add_products([sums_in[k] for k in range(1, 4)], tiles, u_ref, r_ref, img_ref)
            for k, value in enumerate(sums):
                sums_ref[k] = value

        @pl.when(il % 2 == 0)
        def _():
            @pl.when(il > 0)
            def _():
                w = odd_ref[...]
                img_ref[0] += w * w * (u_ref[0] - g_ref[...])

            add(0)

        @pl.when(il % 2 == 1)
        def _():
            @pl.when(il < n_il - 1)
            def _():
                img_ref[rows - 1] += lower_flux(w_ref[rows - 1], odd_ref[...], own_ref[...], sil_ref[rows - 1])

            add(rows - 1)

        lane = lax.broadcasted_iota(jnp.int32, (1, 128), 1)
        row = jnp.zeros((1, 128), jnp.float32)
        for k, value in enumerate([sums_in[0]] + [sums_ref[k] for k in range(3)]):
            value = sum(value[:, j : j + 128] for j in range(128, steps, 128)) + value[:, :128]
            value = jnp.sum(jnp.sum(value, axis=0, keepdims=True), axis=1, keepdims=True)
            row = jnp.where(lane == k, value, row)
        out_ref[...] = jnp.broadcast_to(row, (n_dev, 128))

    return pl.pallas_call(
        kernel,
        in_specs=[VMEM] * (10 + 2 * len(xl_parities)),
        out_specs=[VMEM, VMEM],
        out_shape=[f32(rows, cols, steps), f32(n_dev, 128)],
        input_output_aliases={5: 0},
        scratch_shapes=[pltpu.VMEM((3, 8, steps), jnp.float32)],
        compiler_params=params(),
        name="edges",
    )


def make_update(rows, cols, steps):
    piece = 64 if cols % 64 == 0 else cols

    def kernel(sums_ref, x_ref, r_ref, u_ref, img_ref, x_hbm, r_hbm, d_hbm, x_out, r_out, d_out, sems):
        total = jnp.sum(sums_ref[...], axis=0, keepdims=True)
        lane = lax.broadcasted_iota(jnp.int32, total.shape, 1)
        norm_old, along, cross, square = (
            jnp.sum(jnp.where(lane == k, total, 0.0), axis=1, keepdims=True) for k in range(4)
        )
        alpha = norm_old / along
        norm_new = norm_old - 2.0 * alpha * cross + alpha * alpha * square
        beta = norm_new / norm_old
        copies = []
        pieces = [(i, pl.ds(j, piece)) for i in range(rows) for j in range(0, cols, piece)]
        for n, at in enumerate(pieces):
            u = u_ref[at]
            residual = r_ref[at] - alpha * img_ref[at]
            x_out[at] = x_ref[at] + alpha * u
            r_out[at] = residual
            d_out[at] = residual + beta * u
            for k, (src, dst) in enumerate(((x_out, x_hbm), (r_out, r_hbm), (d_out, d_hbm))):
                copy = pltpu.make_async_copy(src.at[at], dst.at[at], sems.at[k, n])
                copy.start()
                copies.append(copy)
        for copy in copies:
            copy.wait()

    return pl.pallas_call(
        kernel,
        in_specs=[VMEM] * 5,
        out_specs=[HBM] * 3,
        out_shape=[f32(rows, cols, steps)] * 3,
        scratch_shapes=[pltpu.VMEM((rows, cols, steps), jnp.float32)] * 3
        + [pltpu.SemaphoreType.DMA((3, rows * cols // piece))],
        compiler_params=params(),
        name="update",
    )


def solution(mesh):
    n_il, n_xl = mesh.shape["il"], mesh.shape["xl"]
    n_dev = n_il * n_xl
    axes = ("il", "xl")
    even_swap, odd_swap = (swap_pairs((n_il, n_xl), 0, parity)[0] for parity in range(2))
    up = [(i, (i + 1) % n_il) for i in range(n_il)]
    xl_swaps = [swap_pairs((n_il, n_xl), 1, parity) for parity in range(2)]
    xl_parities = [parity for parity in range(2) if xl_swaps[parity][1]]

    def step(x, r, u, s_il, s_xl, w):
        rows, cols, steps = u.shape
        stay = [pltpu.with_memory_space_constraint(a, pltpu.HBM) for a in (u, s_il)]
        g = make_slope_row(rows, cols, steps)(stay[0], stay[1])
        g_got = lax.ppermute(g, "il", up)
        odd_sent = make_pick(rows, cols, steps)(g, u, w)
        odd = lax.ppermute(odd_sent, axes, odd_swap)
        xl_sent = make_pack(rows, cols, steps, xl_parities)(odd_sent, u, s_xl, w)
        xl_got = []
        for p, buf in zip(xl_parities, xl_sent):
            xl_got.append(lax.ppermute(buf, axes, xl_swaps[p][0]))
        even_sent = make_pair(rows, cols, steps)(xl_sent[0] if xl_sent else odd_sent, u, s_il, w)
        even = lax.ppermute(even_sent, axes, even_swap)
        part, sums = make_inner(rows, cols, steps)(u, r, s_il, s_xl, w)
        part, sums = make_even_edge(rows, cols, steps, n_il)(u, r, s_il, w, even_sent, even, even_sent, part, sums)
        image, row = make_edges(rows, cols, steps, n_il, n_xl, xl_parities, n_dev)(
            u, r, s_il, s_xl, w, part, sums, g, odd, g_got, *xl_sent, *xl_got
        )
        rows_all = lax.all_to_all(row, axes, 0, 0, tiled=True)
        return make_update(rows, cols, steps)(rows_all, x, r, u, image)

    placed = P("il", "xl", None)
    return jax.shard_map(step, mesh=mesh, in_specs=(placed,) * 6, out_specs=(placed,) * 3, check_vma=False)
```

```python
import jax
import jax.numpy as jnp
from jax import lax
from jax.experimental import pallas as pl
from jax.experimental.pallas import tpu as pltpu
from jax.sharding import PartitionSpec as P


damping = 0.3
VMEM_LIMIT = 16 * 1024 * 1024


def swap_pairs(sizes, axis, parity):
    n_il, n_xl = sizes
    size, other = (n_il, n_xl) if axis == 0 else (n_xl, n_il)
    pairs, real = [], False
    for a in range(size):
        mate = a + 1 if a % 2 == parity else a - 1
        inside = 0 <= mate < size
        real = real or inside
        for b in range(other):
            if inside:
                a_to, b_to = mate, b
            else:
                a_to, b_to = a, (b ^ 1 if (b ^ 1) < other else b)
            here, there = ((a, b), (a_to, b_to)) if axis == 0 else ((b, a), (b_to, a_to))
            pairs.append((here[0] * n_xl + here[1], there[0] * n_xl + there[1]))
    return pairs, real


def time_diff(field):
    steps = field.shape[-1]
    at = lax.broadcasted_iota(jnp.int32, field.shape, field.ndim - 1)
    after = jnp.where(at == steps - 1, 0.0, pltpu.roll(field, steps - 1, field.ndim - 1))
    before = jnp.where(at == 0, 0.0, pltpu.roll(field, 1, field.ndim - 1))
    return 0.5 * (after - before)


def params():
    return pltpu.CompilerParams(vmem_limit_bytes=VMEM_LIMIT)


VMEM = pl.BlockSpec(memory_space=pltpu.VMEM)
HBM = pl.BlockSpec(memory_space=pltpu.HBM)


def f32(*shape):
    return jax.ShapeDtypeStruct(shape, jnp.float32)


def make_rows(rows, cols, steps):
    def kernel(w_hbm, sil_hbm, w_row, s_row, sems):
        @pl.when(lax.axis_index("il") % 2 == 1)
        def _():
            pairs = ((w_hbm, w_row), (sil_hbm, s_row))
            copies = [pltpu.make_async_copy(src.at[rows - 1], dst, sems.at[k]) for k, (src, dst) in enumerate(pairs)]
            for copy in copies:
                copy.start()
            for copy in copies:
                copy.wait()

    return pl.pallas_call(
        kernel,
        in_specs=[HBM] * 2,
        out_specs=[VMEM] * 2,
        out_shape=[f32(cols, steps)] * 2,
        scratch_shapes=[pltpu.SemaphoreType.DMA((2,))],
        compiler_params=params(),
        name="rows",
    )


def make_pick(rows, cols, steps):
    def kernel(u_ref, s_row, odd_ref):
        il_odd = lax.axis_index("il") % 2

        @pl.when(il_odd == 0)
        def _():
            odd_ref[...] = u_ref[0]

        @pl.when(il_odd == 1)
        def _():
            u = u_ref[rows - 1]
            odd_ref[...] = u + s_row[...] * time_diff(u)

    return pl.pallas_call(
        kernel,
        in_specs=[VMEM, VMEM],
        out_specs=VMEM,
        out_shape=f32(cols, steps),
        compiler_params=params(),
        name="pick",
    )


def make_pack(rows, cols, steps, xl_parities):
    def kernel(_, u_ref, sxl_ref, w_ref, *bufs):
        xl_odd = lax.axis_index("xl") % 2
        u = u_ref[:, cols - 1, :]
        g = u + sxl_ref[:, cols - 1, :] * time_diff(u)
        for parity, buf in zip(xl_parities, bufs):
            buf[pl.ds(rows, rows)] = g

            @pl.when(xl_odd == parity)
            def _(buf=buf):
                buf[pl.ds(0, rows)] = w_ref[:, cols - 1, :]

            @pl.when(xl_odd != parity)
            def _(buf=buf):
                buf[pl.ds(0, rows)] = u_ref[:, 0, :]

    return pl.pallas_call(
        kernel,
        in_specs=[pl.BlockSpec(memory_space=pl.ANY)] + [VMEM] * 3,
        out_specs=[VMEM] * len(xl_parities),
        out_shape=[f32(2 * rows, steps)] * len(xl_parities),
        compiler_params=params(),
        name="pack",
    )


def make_pair(rows, cols, steps):
    def kernel(_, u_ref, sil_ref, w_ref, even_ref):
        il_odd = lax.axis_index("il") % 2

        @pl.when(il_odd == 0)
        def _():
            u = u_ref[rows - 1]
            even_ref[0] = w_ref[rows - 1]
            even_ref[1] = u + sil_ref[rows - 1] * time_diff(u)

        @pl.when(il_odd == 1)
        def _():
            even_ref[0] = u_ref[0]

    return pl.pallas_call(
        kernel,
        in_specs=[pl.BlockSpec(memory_space=pl.ANY)] + [VMEM] * 3,
        out_specs=VMEM,
        out_shape=f32(2, cols, steps),
        compiler_params=params(),
        name="pair",
    )


def edge_tiles(cols):
    return sorted({0, cols - 8})


def inner_tiles(cols):
    return range(8, cols - 8, 8)


def add_products(sums, tiles, u_ref, r_ref, img_ref):
    for i, j in tiles:
        at = (i, pl.ds(j, 8))
        u, r, image = u_ref[at], r_ref[at], img_ref[at]
        sums = [s + a * b for s, (a, b) in zip(sums, ((u, image), (r, image), (image, image)))]
    return sums


def lower_flux(w, ahead, g, slope):
    flux = w * w * (ahead - g)
    return time_diff(slope * flux) - flux


def make_inner(rows, cols, steps):
    def kernel(u_ref, r_ref, sil_ref, sxl_ref, w_ref, img_ref, sums_ref):
        col = lax.broadcasted_iota(jnp.int32, (cols, steps), 0)
        flux_before = None
        norm = jnp.zeros((8, steps), jnp.float32)
        sums = [norm] * 3
        for i in range(rows):
            u = u_ref[i]
            w2 = w_ref[i] * w_ref[i]
            slope_t = time_diff(u)
            s_xl = sxl_ref[i]
            ahead = pltpu.roll(u, cols - 1, 0)
            flux_xl = jnp.where(col == cols - 1, 0.0, w2 * (ahead - u - s_xl * slope_t))
            behind = jnp.where(col == 0, 0.0, pltpu.roll(flux_xl, 1, 0))
            image = behind - flux_xl + damping * u
            along = s_xl * flux_xl
            if flux_before is not None:
                image = image + flux_before
            if i < rows - 1:
                s_il = sil_ref[i]
                flux_il = w2 * (u_ref[i + 1] - u - s_il * slope_t)
                image = image - flux_il
                along = along + s_il * flux_il
                flux_before = flux_il
            img_ref[i] = image + time_diff(along)
            for j in range(0, cols, 8):
                r = r_ref[i, pl.ds(j, 8)]
                norm = norm + r * r
            if 0 < i < rows - 1:
                sums = add_products(sums, [(i, j) for j in inner_tiles(cols)], u_ref, r_ref, img_ref)
        for k, value in enumerate([norm] + sums):
            sums_ref[k] = value

    return pl.pallas_call(
        kernel,
        in_specs=[VMEM] * 5,
        out_specs=[VMEM] * 2,
        out_shape=[f32(rows, cols, steps), f32(4, 8, steps)],
        compiler_params=params(),
        name="inner",
    )


def make_near_edges(rows, cols, steps, n_il, n_xl, xl_parities):
    half = len(xl_parities)

    def kernel(u_ref, r_ref, sil_ref, sxl_ref, w_ref, img_in, sums_in, mine_ref, got_ref, *rest):
        bufs = rest[:-2]
        img_ref, sums_ref = rest[-2:]
        il, xl = lax.axis_index("il"), lax.axis_index("xl")

        for parity, mine, got in zip(xl_parities, bufs[:half], bufs[half:]):

            @pl.when((xl % 2 == parity) & (xl < n_xl - 1))
            def _(mine=mine, got=got):
                here, there = pl.ds(0, rows), pl.ds(rows, rows)
                add = lower_flux(mine[here], got[here], mine[there], sxl_ref[:, cols - 1, :])
                for i in range(rows):
                    img_ref[i, pl.ds(cols - 1, 1), :] += add[i : i + 1]

            @pl.when((xl % 2 != parity) & (xl > 0))
            def _(got=got):
                w = got[pl.ds(0, rows)]
                add = w * w * (u_ref[:, 0, :] - got[pl.ds(rows, rows)])
                for i in range(rows):
                    img_ref[i, pl.ds(0, 1), :] += add[i : i + 1]

        def add_row(row):
            tiles = [(row, j) for j in range(0, cols, 8)] if rows > 1 else []
            tiles += [(i, j) for i in range(1, rows - 1) for j in edge_tiles(cols)]
            sums = add_products([sums_ref[k] for k in range(1, 4)], tiles, u_ref, r_ref, img_ref)
            for k, value in enumerate(sums):
                sums_ref[k + 1] = value

        @pl.when(il % 2 == 0)
        def _():
            @pl.when(il < n_il - 1)
            def _():
                img_ref[rows - 1] += lower_flux(w_ref[rows - 1], got_ref[0], mine_ref[1], sil_ref[rows - 1])

            add_row(rows - 1)

        @pl.when(il % 2 == 1)
        def _():
            img_ref[0] += got_ref[0] * got_ref[0] * (u_ref[0] - got_ref[1])
            add_row(0)

    return pl.pallas_call(
        kernel,
        in_specs=[VMEM] * (9 + 2 * half),
        out_specs=[VMEM] * 2,
        out_shape=[f32(rows, cols, steps), f32(4, 8, steps)],
        input_output_aliases={5: 0, 6: 1},
        compiler_params=params(),
        name="near_edges",
    )


def make_edges(rows, cols, steps, n_il, n_dev):
    def kernel(u_ref, r_ref, sil_ref, w_ref, img_in, sums_in, own_ref, odd_ref, w_got_ref, img_ref, out_ref, sums_ref):
        il = lax.axis_index("il")

        def add_row(row):
            tiles = [(row, j) for j in range(0, cols, 8)]
            sums = add_products([sums_in[k] for k in range(1, 4)], tiles, u_ref, r_ref, img_ref)
            for k, value in enumerate([sums_in[0]] + sums):
                value = sum(value[:, j : j + 128] for j in range(128, steps, 128)) + value[:, :128]
                sums_ref[pl.ds(k, 1)] = jnp.sum(value, axis=0, keepdims=True)

        @pl.when(il % 2 == 0)
        def _():
            @pl.when(il > 0)
            def _():
                w = w_got_ref[...]
                img_ref[0] += w * w * (u_ref[0] - odd_ref[...])

            add_row(0)

        @pl.when(il % 2 == 1)
        def _():
            @pl.when(il < n_il - 1)
            def _():
                img_ref[rows - 1] += lower_flux(w_ref[rows - 1], odd_ref[...], own_ref[...], sil_ref[rows - 1])

            add_row(rows - 1)

        lane = lax.broadcasted_iota(jnp.int32, (1, 128), 1)
        row = jnp.zeros((1, 128), jnp.float32)
        for k in range(4):
            row = jnp.where(lane == k, jnp.sum(sums_ref[pl.ds(k, 1)], axis=1, keepdims=True), row)
        out_ref[...] = jnp.broadcast_to(row, (n_dev, 128))

    return pl.pallas_call(
        kernel,
        in_specs=[VMEM] * 9,
        out_specs=[VMEM, VMEM],
        out_shape=[f32(rows, cols, steps), f32(n_dev, 128)],
        input_output_aliases={4: 0},
        scratch_shapes=[pltpu.VMEM((4, 128), jnp.float32)],
        compiler_params=params(),
        name="edges",
    )


def make_update(rows, cols, steps):
    piece = 64 if cols % 64 == 0 else cols

    def kernel(sums_ref, x_ref, r_ref, u_ref, img_ref, x_hbm, r_hbm, d_hbm, x_out, r_out, d_out, sems):
        total = jnp.sum(sums_ref[...], axis=0, keepdims=True)
        lane = lax.broadcasted_iota(jnp.int32, total.shape, 1)
        norm_old, along, cross, square = (
            jnp.sum(jnp.where(lane == k, total, 0.0), axis=1, keepdims=True) for k in range(4)
        )
        alpha = norm_old / along
        norm_new = norm_old - 2.0 * alpha * cross + alpha * alpha * square
        beta = norm_new / norm_old
        copies = []
        pieces = [(i, pl.ds(j, piece)) for i in range(rows) for j in range(0, cols, piece)]
        for n, at in enumerate(pieces):
            u = u_ref[at]
            residual = r_ref[at] - alpha * img_ref[at]
            x_out[at] = x_ref[at] + alpha * u
            r_out[at] = residual
            d_out[at] = residual + beta * u
            for k, (src, dst) in enumerate(((x_out, x_hbm), (r_out, r_hbm), (d_out, d_hbm))):
                copy = pltpu.make_async_copy(src.at[at], dst.at[at], sems.at[k, n])
                copy.start()
                copies.append(copy)
        for copy in copies:
            copy.wait()

    return pl.pallas_call(
        kernel,
        in_specs=[VMEM] * 5,
        out_specs=[HBM] * 3,
        out_shape=[f32(rows, cols, steps)] * 3,
        scratch_shapes=[pltpu.VMEM((rows, cols, steps), jnp.float32)] * 3
        + [pltpu.SemaphoreType.DMA((3, rows * cols // piece))],
        compiler_params=params(),
        name="update",
    )


def solution(mesh):
    n_il, n_xl = mesh.shape["il"], mesh.shape["xl"]
    n_dev = n_il * n_xl
    axes = ("il", "xl")
    even_swap, odd_swap = (swap_pairs((n_il, n_xl), 0, parity)[0] for parity in range(2))
    up = [(i, (i + 1) % n_il) for i in range(n_il)]
    xl_swaps = [swap_pairs((n_il, n_xl), 1, parity) for parity in range(2)]
    xl_parities = [parity for parity in range(2) if xl_swaps[parity][1]]

    def step(x, r, u, s_il, s_xl, w):
        rows, cols, steps = u.shape
        stay = [pltpu.with_memory_space_constraint(a, pltpu.HBM) for a in (w, s_il)]
        w_sent, s_row = make_rows(rows, cols, steps)(*stay)
        w_got = lax.ppermute(w_sent, "il", up)
        odd_sent = make_pick(rows, cols, steps)(u, s_row)
        odd = lax.ppermute(odd_sent, axes, odd_swap)
        xl_sent = make_pack(rows, cols, steps, xl_parities)(odd_sent, u, s_xl, w)
        xl_got = []
        for p, buf in zip(xl_parities, xl_sent):
            xl_got.append(lax.ppermute(buf, axes, xl_swaps[p][0]))
        even_sent = make_pair(rows, cols, steps)(xl_sent[0] if xl_sent else odd_sent, u, s_il, w)
        even = lax.ppermute(even_sent, axes, even_swap)
        part, sums = make_inner(rows, cols, steps)(u, r, s_il, s_xl, w)
        part, sums = make_near_edges(rows, cols, steps, n_il, n_xl, xl_parities)(
            u, r, s_il, s_xl, w, part, sums, even_sent, even, *xl_sent, *xl_got
        )
        image, row = make_edges(rows, cols, steps, n_il, n_dev)(u, r, s_il, w, part, sums, odd_sent, odd, w_got)
        rows_all = lax.all_to_all(row, axes, 0, 0, tiled=True)
        return make_update(rows, cols, steps)(rows_all, x, r, u, image)

    placed = P("il", "xl", None)
    return jax.shard_map(step, mesh=mesh, in_specs=(placed,) * 6, out_specs=(placed,) * 3, check_vma=False)
```

```python
import jax
import jax.numpy as jnp
from jax import lax
from jax.experimental import pallas as pl
from jax.experimental.pallas import tpu as pltpu
from jax.sharding import PartitionSpec as P


damping = 0.3
VMEM_LIMIT = 16 * 1024 * 1024


def swap_pairs(sizes, axis, parity):
    n_il, n_xl = sizes
    size, other = (n_il, n_xl) if axis == 0 else (n_xl, n_il)
    pairs, real = [], False
    for a in range(size):
        mate = a + 1 if a % 2 == parity else a - 1
        inside = 0 <= mate < size
        real = real or inside
        for b in range(other):
            if inside:
                a_to, b_to = mate, b
            else:
                a_to, b_to = a, (b ^ 1 if (b ^ 1) < other else b)
            here, there = ((a, b), (a_to, b_to)) if axis == 0 else ((b, a), (b_to, a_to))
            pairs.append((here[0] * n_xl + here[1], there[0] * n_xl + there[1]))
    return pairs, real


def time_diff(field):
    steps = field.shape[-1]
    at = lax.broadcasted_iota(jnp.int32, field.shape, field.ndim - 1)
    after = jnp.where(at == steps - 1, 0.0, pltpu.roll(field, steps - 1, field.ndim - 1))
    before = jnp.where(at == 0, 0.0, pltpu.roll(field, 1, field.ndim - 1))
    return 0.5 * (after - before)


def params():
    return pltpu.CompilerParams(vmem_limit_bytes=VMEM_LIMIT)


VMEM = pl.BlockSpec(memory_space=pltpu.VMEM)
HBM = pl.BlockSpec(memory_space=pltpu.HBM)


def f32(*shape):
    return jax.ShapeDtypeStruct(shape, jnp.float32)


def make_slope_row(rows, cols, steps):
    def kernel(u_hbm, sil_hbm, g_ref, u_ref, s_ref, sems):
        @pl.when(lax.axis_index("il") % 2 == 1)
        def _():
            pairs = ((u_hbm.at[rows - 1], u_ref), (sil_hbm.at[rows - 1], s_ref))
            copies = [pltpu.make_async_copy(src, dst, sems.at[k]) for k, (src, dst) in enumerate(pairs)]
            for copy in copies:
                copy.start()
            for copy in copies:
                copy.wait()
            u = u_ref[...]
            g_ref[...] = u + s_ref[...] * time_diff(u)

    return pl.pallas_call(
        kernel,
        in_specs=[HBM] * 2,
        out_specs=VMEM,
        out_shape=f32(cols, steps),
        scratch_shapes=[pltpu.VMEM((cols, steps), jnp.float32)] * 2 + [pltpu.SemaphoreType.DMA((2,))],
        compiler_params=params(),
        name="slope_row",
    )


def make_pick(rows, cols, steps):
    def kernel(_, u_ref, w_ref, odd_ref):
        il_odd = lax.axis_index("il") % 2

        @pl.when(il_odd == 0)
        def _():
            odd_ref[...] = u_ref[0]

        @pl.when(il_odd == 1)
        def _():
            odd_ref[...] = w_ref[rows - 1]

    return pl.pallas_call(
        kernel,
        in_specs=[pl.BlockSpec(memory_space=pl.ANY), VMEM, VMEM],
        out_specs=VMEM,
        out_shape=f32(cols, steps),
        compiler_params=params(),
        name="pick",
    )


def make_pack(rows, cols, steps, xl_parities):
    def kernel(_, u_ref, sxl_ref, w_ref, *bufs):
        xl_odd = lax.axis_index("xl") % 2
        u = u_ref[:, cols - 1, :]
        g = u + sxl_ref[:, cols - 1, :] * time_diff(u)
        for parity, buf in zip(xl_parities, bufs):
            buf[pl.ds(rows, rows)] = g

            @pl.when(xl_odd == parity)
            def _(buf=buf):
                buf[pl.ds(0, rows)] = w_ref[:, cols - 1, :]

            @pl.when(xl_odd != parity)
            def _(buf=buf):
                buf[pl.ds(0, rows)] = u_ref[:, 0, :]

    return pl.pallas_call(
        kernel,
        in_specs=[pl.BlockSpec(memory_space=pl.ANY)] + [VMEM] * 3,
        out_specs=[VMEM] * len(xl_parities),
        out_shape=[f32(2 * rows, steps)] * len(xl_parities),
        compiler_params=params(),
        name="pack",
    )


def make_pair(rows, cols, steps):
    def kernel(_, u_ref, sil_ref, w_ref, even_ref):
        il_odd = lax.axis_index("il") % 2

        @pl.when(il_odd == 0)
        def _():
            u = u_ref[rows - 1]
            even_ref[0] = w_ref[rows - 1]
            even_ref[1] = u + sil_ref[rows - 1] * time_diff(u)

        @pl.when(il_odd == 1)
        def _():
            even_ref[0] = u_ref[0]

    return pl.pallas_call(
        kernel,
        in_specs=[pl.BlockSpec(memory_space=pl.ANY)] + [VMEM] * 3,
        out_specs=VMEM,
        out_shape=f32(2, cols, steps),
        compiler_params=params(),
        name="pair",
    )


def edge_tiles(cols):
    return sorted({0, cols - 8})


def inner_tiles(cols):
    return range(8, cols - 8, 8)


def add_products(sums, tiles, u_ref, r_ref, img_ref):
    for i, j in tiles:
        at = (i, pl.ds(j, 8))
        u, r, image = u_ref[at], r_ref[at], img_ref[at]
        sums = [s + a * b for s, (a, b) in zip(sums, ((u, image), (r, image), (image, image)))]
    return sums


def lower_flux(w, ahead, g, slope):
    flux = w * w * (ahead - g)
    return time_diff(slope * flux) - flux


def make_inner(rows, cols, steps):
    def kernel(u_ref, r_ref, sil_ref, sxl_ref, w_ref, img_ref, sums_ref):
        col = lax.broadcasted_iota(jnp.int32, (cols, steps), 0)
        flux_before = None
        norm = jnp.zeros((8, steps), jnp.float32)
        sums = [norm] * 3
        for i in range(rows):
            u = u_ref[i]
            w2 = w_ref[i] * w_ref[i]
            slope_t = time_diff(u)
            s_xl = sxl_ref[i]
            ahead = pltpu.roll(u, cols - 1, 0)
            flux_xl = jnp.where(col == cols - 1, 0.0, w2 * (ahead - u - s_xl * slope_t))
            behind = jnp.where(col == 0, 0.0, pltpu.roll(flux_xl, 1, 0))
            image = behind - flux_xl + damping * u
            along = s_xl * flux_xl
            if flux_before is not None:
                image = image + flux_before
            if i < rows - 1:
                s_il = sil_ref[i]
                flux_il = w2 * (u_ref[i + 1] - u - s_il * slope_t)
                image = image - flux_il
                along = along + s_il * flux_il
                flux_before = flux_il
            img_ref[i] = image + time_diff(along)
            for j in range(0, cols, 8):
                r = r_ref[i, pl.ds(j, 8)]
                norm = norm + r * r
            if 0 < i < rows - 1:
                sums = add_products(sums, [(i, j) for j in inner_tiles(cols)], u_ref, r_ref, img_ref)
        for k, value in enumerate([norm] + sums):
            sums_ref[k] = value

    return pl.pallas_call(
        kernel,
        in_specs=[VMEM] * 5,
        out_specs=[VMEM] * 2,
        out_shape=[f32(rows, cols, steps), f32(4, 8, steps)],
        compiler_params=params(),
        name="inner",
    )


def make_even_edge(rows, cols, steps, n_il):
    def kernel(u_ref, r_ref, sil_ref, w_ref, mine_ref, got_ref, _, img_in, sums_in, img_ref, sums_ref):
        il = lax.axis_index("il")

        def add(row):
            if rows > 1:
                sums = add_products(
                    [sums_ref[k] for k in range(1, 4)], [(row, j) for j in inner_tiles(cols)], u_ref, r_ref, img_ref
                )
                for k, value in enumerate(sums):
                    sums_ref[k + 1] = value

        @pl.when(il % 2 == 0)
        def _():
            @pl.when(il < n_il - 1)
            def _():
                img_ref[rows - 1] += lower_flux(w_ref[rows - 1], got_ref[0], mine_ref[1], sil_ref[rows - 1])

            add(rows - 1)

        @pl.when(il % 2 == 1)
        def _():
            img_ref[0] += got_ref[0] * got_ref[0] * (u_ref[0] - got_ref[1])
            add(0)

    return pl.pallas_call(
        kernel,
        in_specs=[VMEM] * 6 + [pl.BlockSpec(memory_space=pl.ANY)] + [VMEM] * 2,
        out_specs=[VMEM] * 2,
        out_shape=[f32(rows, cols, steps), f32(4, 8, steps)],
        input_output_aliases={7: 0, 8: 1},
        compiler_params=params(),
        name="even_edge",
    )


def make_edges(rows, cols, steps, n_il, n_xl, xl_parities, n_dev):
    def kernel(u_ref, r_ref, sil_ref, sxl_ref, w_ref, part_ref, sums_in, own_ref, odd_ref, g_ref, *rest):
        bufs = rest[:-3]
        img_ref, out_ref, sums_ref = rest[-3:]
        il, xl = lax.axis_index("il"), lax.axis_index("xl")

        half = len(xl_parities)
        for parity, mine, got in zip(xl_parities, bufs[:half], bufs[half:]):

            @pl.when((xl % 2 == parity) & (xl < n_xl - 1))
            def _(mine=mine, got=got):
                here, there = pl.ds(0, rows), pl.ds(rows, rows)
                add = lower_flux(mine[here], got[here], mine[there], sxl_ref[:, cols - 1, :])
                for i in range(rows):
                    img_ref[i, pl.ds(cols - 1, 1), :] += add[i : i + 1]

            @pl.when((xl % 2 != parity) & (xl > 0))
            def _(got=got):
                w = got[pl.ds(0, rows)]
                add = w * w * (u_ref[:, 0, :] - got[pl.ds(rows, rows)])
                for i in range(rows):
                    img_ref[i, pl.ds(0, 1), :] += add[i : i + 1]

        def add(row):
            tiles = [(row, j) for j in inner_tiles(cols)]
            tiles += [(i, j) for i in range(rows) for j in edge_tiles(cols)]
            sums = add_products([sums_in[k] for k in range(1, 4)], tiles, u_ref, r_ref, img_ref)
            for k, value in enumerate(sums):
                sums_ref[k] = value

        @pl.when(il % 2 == 0)
        def _():
            @pl.when(il > 0)
            def _():
                w = odd_ref[...]
                img_ref[0] += w * w * (u_ref[0] - g_ref[...])

            add(0)

        @pl.when(il % 2 == 1)
        def _():
            @pl.when(il < n_il - 1)
            def _():
                img_ref[rows - 1] += lower_flux(w_ref[rows - 1], odd_ref[...], own_ref[...], sil_ref[rows - 1])

            add(rows - 1)

        lane = lax.broadcasted_iota(jnp.int32, (1, 128), 1)
        row = jnp.zeros((1, 128), jnp.float32)
        for k, value in enumerate([sums_in[0]] + [sums_ref[k] for k in range(3)]):
            value = sum(value[:, j : j + 128] for j in range(128, steps, 128)) + value[:, :128]
            value = jnp.sum(value, axis=0, keepdims=True)
            value = value + pltpu.roll(value, 64, 1)
            row = jnp.where(lane // 32 == k, value + pltpu.roll(value, 32, 1), row)
        out_ref[...] = jnp.broadcast_to(row, (n_dev, 128))

    return pl.pallas_call(
        kernel,
        in_specs=[VMEM] * (10 + 2 * len(xl_parities)),
        out_specs=[VMEM, VMEM],
        out_shape=[f32(rows, cols, steps), f32(n_dev, 128)],
        input_output_aliases={5: 0},
        scratch_shapes=[pltpu.VMEM((3, 8, steps), jnp.float32)],
        compiler_params=params(),
        name="edges",
    )


def make_update(rows, cols, steps):
    piece = 64 if cols % 64 == 0 else cols

    def kernel(sums_ref, x_ref, r_ref, u_ref, img_ref, x_hbm, r_hbm, d_hbm, x_out, r_out, d_out, sems):
        total = jnp.sum(sums_ref[...], axis=0, keepdims=True)
        lane = lax.broadcasted_iota(jnp.int32, total.shape, 1)
        norm_old, along, cross, square = (
            jnp.sum(jnp.where(lane // 32 == k, total, 0.0), axis=1, keepdims=True) for k in range(4)
        )
        alpha = norm_old / along
        norm_new = norm_old - 2.0 * alpha * cross + alpha * alpha * square
        beta = norm_new / norm_old
        copies = []
        pieces = [(i, pl.ds(j, piece)) for i in range(rows) for j in range(0, cols, piece)]
        for n, at in enumerate(pieces):
            u = u_ref[at]
            residual = r_ref[at] - alpha * img_ref[at]
            x_out[at] = x_ref[at] + alpha * u
            r_out[at] = residual
            d_out[at] = residual + beta * u
            for k, (src, dst) in enumerate(((x_out, x_hbm), (r_out, r_hbm), (d_out, d_hbm))):
                copy = pltpu.make_async_copy(src.at[at], dst.at[at], sems.at[k, n])
                copy.start()
                copies.append(copy)
        for copy in copies:
            copy.wait()

    return pl.pallas_call(
        kernel,
        in_specs=[VMEM] * 5,
        out_specs=[HBM] * 3,
        out_shape=[f32(rows, cols, steps)] * 3,
        scratch_shapes=[pltpu.VMEM((rows, cols, steps), jnp.float32)] * 3
        + [pltpu.SemaphoreType.DMA((3, rows * cols // piece))],
        compiler_params=params(),
        name="update",
    )


def solution(mesh):
    n_il, n_xl = mesh.shape["il"], mesh.shape["xl"]
    n_dev = n_il * n_xl
    axes = ("il", "xl")
    even_swap, odd_swap = (swap_pairs((n_il, n_xl), 0, parity)[0] for parity in range(2))
    up = [(i, (i + 1) % n_il) for i in range(n_il)]
    xl_swaps = [swap_pairs((n_il, n_xl), 1, parity) for parity in range(2)]
    xl_parities = [parity for parity in range(2) if xl_swaps[parity][1]]

    def step(x, r, u, s_il, s_xl, w):
        rows, cols, steps = u.shape
        stay = [pltpu.with_memory_space_constraint(a, pltpu.HBM) for a in (u, s_il)]
        g = make_slope_row(rows, cols, steps)(stay[0], stay[1])
        g_got = lax.ppermute(g, "il", up)
        odd_sent = make_pick(rows, cols, steps)(g, u, w)
        odd = lax.ppermute(odd_sent, axes, odd_swap)
        xl_sent = make_pack(rows, cols, steps, xl_parities)(odd_sent, u, s_xl, w)
        xl_got = []
        for p, buf in zip(xl_parities, xl_sent):
            xl_got.append(lax.ppermute(buf, axes, xl_swaps[p][0]))
        even_sent = make_pair(rows, cols, steps)(xl_sent[0] if xl_sent else odd_sent, u, s_il, w)
        even = lax.ppermute(even_sent, axes, even_swap)
        part, sums = make_inner(rows, cols, steps)(u, r, s_il, s_xl, w)
        part, sums = make_even_edge(rows, cols, steps, n_il)(u, r, s_il, w, even_sent, even, even_sent, part, sums)
        image, row = make_edges(rows, cols, steps, n_il, n_xl, xl_parities, n_dev)(
            u, r, s_il, s_xl, w, part, sums, g, odd, g_got, *xl_sent, *xl_got
        )
        rows_all = lax.all_to_all(row, axes, 0, 0, tiled=True)
        return make_update(rows, cols, steps)(rows_all, x, r, u, image)

    placed = P("il", "xl", None)
    return jax.shard_map(step, mesh=mesh, in_specs=(placed,) * 6, out_specs=(placed,) * 3, check_vma=False)
```

```python
import jax
import jax.numpy as jnp
from jax import lax
from jax.experimental import pallas as pl
from jax.experimental.pallas import tpu as pltpu
from jax.sharding import PartitionSpec as P


damping = 0.3
VMEM_LIMIT = 16 * 1024 * 1024


def swap_pairs(sizes, axis, parity):
    n_il, n_xl = sizes
    size, other = (n_il, n_xl) if axis == 0 else (n_xl, n_il)
    pairs, real = [], False
    for a in range(size):
        mate = a + 1 if a % 2 == parity else a - 1
        inside = 0 <= mate < size
        real = real or inside
        for b in range(other):
            if inside:
                a_to, b_to = mate, b
            else:
                a_to, b_to = a, (b ^ 1 if (b ^ 1) < other else b)
            here, there = ((a, b), (a_to, b_to)) if axis == 0 else ((b, a), (b_to, a_to))
            pairs.append((here[0] * n_xl + here[1], there[0] * n_xl + there[1]))
    return pairs, real


def time_diff(field):
    steps = field.shape[-1]
    at = lax.broadcasted_iota(jnp.int32, field.shape, field.ndim - 1)
    after = jnp.where(at == steps - 1, 0.0, pltpu.roll(field, steps - 1, field.ndim - 1))
    before = jnp.where(at == 0, 0.0, pltpu.roll(field, 1, field.ndim - 1))
    return 0.5 * (after - before)


def params():
    return pltpu.CompilerParams(vmem_limit_bytes=VMEM_LIMIT)


VMEM = pl.BlockSpec(memory_space=pltpu.VMEM)
HBM = pl.BlockSpec(memory_space=pltpu.HBM)


def f32(*shape):
    return jax.ShapeDtypeStruct(shape, jnp.float32)


def make_slope_row(rows, cols, steps):
    def kernel(u_hbm, sil_hbm, g_ref, u_ref, s_ref, sems):
        @pl.when(lax.axis_index("il") % 2 == 1)
        def _():
            pairs = ((u_hbm.at[rows - 1], u_ref), (sil_hbm.at[rows - 1], s_ref))
            copies = [pltpu.make_async_copy(src, dst, sems.at[k]) for k, (src, dst) in enumerate(pairs)]
            for copy in copies:
                copy.start()
            for copy in copies:
                copy.wait()
            u = u_ref[...]
            g_ref[...] = u + s_ref[...] * time_diff(u)

    return pl.pallas_call(
        kernel,
        in_specs=[HBM] * 2,
        out_specs=VMEM,
        out_shape=f32(cols, steps),
        scratch_shapes=[pltpu.VMEM((cols, steps), jnp.float32)] * 2 + [pltpu.SemaphoreType.DMA((2,))],
        compiler_params=params(),
        name="slope_row",
    )


def make_pick(rows, cols, steps):
    def kernel(_, u_ref, w_ref, odd_ref):
        il_odd = lax.axis_index("il") % 2

        @pl.when(il_odd == 0)
        def _():
            odd_ref[...] = u_ref[0]

        @pl.when(il_odd == 1)
        def _():
            odd_ref[...] = w_ref[rows - 1]

    return pl.pallas_call(
        kernel,
        in_specs=[pl.BlockSpec(memory_space=pl.ANY), VMEM, VMEM],
        out_specs=VMEM,
        out_shape=f32(cols, steps),
        compiler_params=params(),
        name="pick",
    )


def make_pack(rows, cols, steps, xl_parities):
    def kernel(_, u_ref, sxl_ref, w_ref, *bufs):
        xl_odd = lax.axis_index("xl") % 2
        u = u_ref[:, cols - 1, :]
        g = u + sxl_ref[:, cols - 1, :] * time_diff(u)
        for parity, buf in zip(xl_parities, bufs):
            buf[pl.ds(rows, rows)] = g

            @pl.when(xl_odd == parity)
            def _(buf=buf):
                buf[pl.ds(0, rows)] = w_ref[:, cols - 1, :]

            @pl.when(xl_odd != parity)
            def _(buf=buf):
                buf[pl.ds(0, rows)] = u_ref[:, 0, :]

    return pl.pallas_call(
        kernel,
        in_specs=[pl.BlockSpec(memory_space=pl.ANY)] + [VMEM] * 3,
        out_specs=[VMEM] * len(xl_parities),
        out_shape=[f32(2 * rows, steps)] * len(xl_parities),
        compiler_params=params(),
        name="pack",
    )


def make_pair(rows, cols, steps):
    def kernel(_, u_ref, sil_ref, w_ref, even_ref):
        il_odd = lax.axis_index("il") % 2

        @pl.when(il_odd == 0)
        def _():
            u = u_ref[rows - 1]
            even_ref[0] = w_ref[rows - 1]
            even_ref[1] = u + sil_ref[rows - 1] * time_diff(u)

        @pl.when(il_odd == 1)
        def _():
            even_ref[0] = u_ref[0]

    return pl.pallas_call(
        kernel,
        in_specs=[pl.BlockSpec(memory_space=pl.ANY)] + [VMEM] * 3,
        out_specs=VMEM,
        out_shape=f32(2, cols, steps),
        compiler_params=params(),
        name="pair",
    )


def edge_tiles(cols):
    return sorted({0, cols - 8})


def inner_tiles(cols):
    return range(8, cols - 8, 8)


def add_products(sums, tiles, u_ref, r_ref, img_ref):
    for i, j in tiles:
        at = (i, pl.ds(j, 8))
        u, r, image = u_ref[at], r_ref[at], img_ref[at]
        sums = [s + a * b for s, (a, b) in zip(sums, ((u, image), (r, image), (image, image)))]
    return sums


def lower_flux(w, ahead, g, slope):
    flux = w * w * (ahead - g)
    return time_diff(slope * flux) - flux


def make_inner(rows, cols, steps):
    def kernel(u_ref, r_ref, sil_ref, sxl_ref, w_ref, img_ref, sums_ref):
        col = lax.broadcasted_iota(jnp.int32, (cols, steps), 0)
        flux_before = None
        norm = jnp.zeros((8, steps), jnp.float32)
        sums = [norm] * 3
        for i in range(rows):
            u = u_ref[i]
            w2 = w_ref[i] * w_ref[i]
            slope_t = time_diff(u)
            s_xl = sxl_ref[i]
            ahead = pltpu.roll(u, cols - 1, 0)
            flux_xl = jnp.where(col == cols - 1, 0.0, w2 * (ahead - u - s_xl * slope_t))
            behind = jnp.where(col == 0, 0.0, pltpu.roll(flux_xl, 1, 0))
            image = behind - flux_xl + damping * u
            along = s_xl * flux_xl
            if flux_before is not None:
                image = image + flux_before
            if i < rows - 1:
                s_il = sil_ref[i]
                flux_il = w2 * (u_ref[i + 1] - u - s_il * slope_t)
                image = image - flux_il
                along = along + s_il * flux_il
                flux_before = flux_il
            img_ref[i] = image + time_diff(along)
            for j in range(0, cols, 8):
                r = r_ref[i, pl.ds(j, 8)]
                norm = norm + r * r
            if 0 < i < rows - 1:
                sums = add_products(sums, [(i, j) for j in inner_tiles(cols)], u_ref, r_ref, img_ref)
        for k, value in enumerate([norm] + sums):
            sums_ref[k] = value

    return pl.pallas_call(
        kernel,
        in_specs=[VMEM] * 5,
        out_specs=[VMEM] * 2,
        out_shape=[f32(rows, cols, steps), f32(4, 8, steps)],
        compiler_params=params(),
        name="inner",
    )


def make_near_edges(rows, cols, steps, n_il, n_xl, xl_parities):
    half = len(xl_parities)

    def kernel(u_ref, r_ref, sil_ref, sxl_ref, w_ref, img_in, sums_in, mine_ref, got_ref, *rest):
        bufs = rest[:-2]
        img_ref, sums_ref = rest[-2:]
        il, xl = lax.axis_index("il"), lax.axis_index("xl")

        for parity, mine, got in zip(xl_parities, bufs[:half], bufs[half:]):

            @pl.when((xl % 2 == parity) & (xl < n_xl - 1))
            def _(mine=mine, got=got):
                here, there = pl.ds(0, rows), pl.ds(rows, rows)
                add = lower_flux(mine[here], got[here], mine[there], sxl_ref[:, cols - 1, :])
                for i in range(rows):
                    img_ref[i, pl.ds(cols - 1, 1), :] += add[i : i + 1]

            @pl.when((xl % 2 != parity) & (xl > 0))
            def _(got=got):
                w = got[pl.ds(0, rows)]
                add = w * w * (u_ref[:, 0, :] - got[pl.ds(rows, rows)])
                for i in range(rows):
                    img_ref[i, pl.ds(0, 1), :] += add[i : i + 1]

        def add_row(row):
            tiles = [(row, j) for j in range(0, cols, 8)] if rows > 1 else []
            tiles += [(i, j) for i in range(1, rows - 1) for j in edge_tiles(cols)]
            sums = add_products([sums_ref[k] for k in range(1, 4)], tiles, u_ref, r_ref, img_ref)
            for k, value in enumerate(sums):
                sums_ref[k + 1] = value

        @pl.when(il % 2 == 0)
        def _():
            @pl.when(il < n_il - 1)
            def _():
                img_ref[rows - 1] += lower_flux(w_ref[rows - 1], got_ref[0], mine_ref[1], sil_ref[rows - 1])

            add_row(rows - 1)

        @pl.when(il % 2 == 1)
        def _():
            img_ref[0] += got_ref[0] * got_ref[0] * (u_ref[0] - got_ref[1])
            add_row(0)

    return pl.pallas_call(
        kernel,
        in_specs=[VMEM] * (9 + 2 * half),
        out_specs=[VMEM] * 2,
        out_shape=[f32(rows, cols, steps), f32(4, 8, steps)],
        input_output_aliases={5: 0, 6: 1},
        compiler_params=params(),
        name="near_edges",
    )


def make_edges(rows, cols, steps, n_il, n_dev):
    def kernel(u_ref, r_ref, sil_ref, w_ref, img_in, sums_in, own_ref, odd_ref, g_ref, img_ref, out_ref, sums_ref):
        il = lax.axis_index("il")

        def add_row(row):
            tiles = [(row, j) for j in range(0, cols, 8)]
            sums = add_products([sums_in[k] for k in range(1, 4)], tiles, u_ref, r_ref, img_ref)
            for k, value in enumerate([sums_in[0]] + sums):
                value = sum(value[:, j : j + 128] for j in range(128, steps, 128)) + value[:, :128]
                sums_ref[pl.ds(k, 1)] = jnp.sum(value, axis=0, keepdims=True)

        @pl.when(il % 2 == 0)
        def _():
            @pl.when(il > 0)
            def _():
                w = odd_ref[...]
                img_ref[0] += w * w * (u_ref[0] - g_ref[...])

            add_row(0)

        @pl.when(il % 2 == 1)
        def _():
            @pl.when(il < n_il - 1)
            def _():
                img_ref[rows - 1] += lower_flux(w_ref[rows - 1], odd_ref[...], own_ref[...], sil_ref[rows - 1])

            add_row(rows - 1)

        lane = lax.broadcasted_iota(jnp.int32, (1, 128), 1)
        row = jnp.zeros((1, 128), jnp.float32)
        for k in range(4):
            row = jnp.where(lane == k, jnp.sum(sums_ref[pl.ds(k, 1)], axis=1, keepdims=True), row)
        out_ref[...] = jnp.broadcast_to(row, (n_dev, 128))

    return pl.pallas_call(
        kernel,
        in_specs=[VMEM] * 9,
        out_specs=[VMEM, VMEM],
        out_shape=[f32(rows, cols, steps), f32(n_dev, 128)],
        input_output_aliases={4: 0},
        scratch_shapes=[pltpu.VMEM((4, 128), jnp.float32)],
        compiler_params=params(),
        name="edges",
    )


def make_update(rows, cols, steps):
    piece = 64 if cols % 64 == 0 else cols

    def kernel(sums_ref, x_ref, r_ref, u_ref, img_ref, x_hbm, r_hbm, d_hbm, x_out, r_out, d_out, sems):
        total = jnp.sum(sums_ref[...], axis=0, keepdims=True)
        lane = lax.broadcasted_iota(jnp.int32, total.shape, 1)
        norm_old, along, cross, square = (
            jnp.sum(jnp.where(lane == k, total, 0.0), axis=1, keepdims=True) for k in range(4)
        )
        alpha = norm_old / along
        norm_new = norm_old - 2.0 * alpha * cross + alpha * alpha * square
        beta = norm_new / norm_old
        copies = []
        pieces = [(i, pl.ds(j, piece)) for i in range(rows) for j in range(0, cols, piece)]
        for n, at in enumerate(pieces):
            u = u_ref[at]
            residual = r_ref[at] - alpha * img_ref[at]
            x_out[at] = x_ref[at] + alpha * u
            r_out[at] = residual
            d_out[at] = residual + beta * u
            for k, (src, dst) in enumerate(((x_out, x_hbm), (r_out, r_hbm), (d_out, d_hbm))):
                copy = pltpu.make_async_copy(src.at[at], dst.at[at], sems.at[k, n])
                copy.start()
                copies.append(copy)
        for copy in copies:
            copy.wait()

    return pl.pallas_call(
        kernel,
        in_specs=[VMEM] * 5,
        out_specs=[HBM] * 3,
        out_shape=[f32(rows, cols, steps)] * 3,
        scratch_shapes=[pltpu.VMEM((rows, cols, steps), jnp.float32)] * 3
        + [pltpu.SemaphoreType.DMA((3, rows * cols // piece))],
        compiler_params=params(),
        name="update",
    )


def solution(mesh):
    n_il, n_xl = mesh.shape["il"], mesh.shape["xl"]
    n_dev = n_il * n_xl
    axes = ("il", "xl")
    even_swap, odd_swap = (swap_pairs((n_il, n_xl), 0, parity)[0] for parity in range(2))
    up = [(i, (i + 1) % n_il) for i in range(n_il)]
    xl_swaps = [swap_pairs((n_il, n_xl), 1, parity) for parity in range(2)]
    xl_parities = [parity for parity in range(2) if xl_swaps[parity][1]]

    def step(x, r, u, s_il, s_xl, w):
        rows, cols, steps = u.shape
        stay = [pltpu.with_memory_space_constraint(a, pltpu.HBM) for a in (u, s_il)]
        g = make_slope_row(rows, cols, steps)(stay[0], stay[1])
        g_got = lax.ppermute(g, "il", up)
        odd_sent = make_pick(rows, cols, steps)(g, u, w)
        odd = lax.ppermute(odd_sent, axes, odd_swap)
        xl_sent = make_pack(rows, cols, steps, xl_parities)(odd_sent, u, s_xl, w)
        xl_got = []
        for p, buf in zip(xl_parities, xl_sent):
            xl_got.append(lax.ppermute(buf, axes, xl_swaps[p][0]))
        even_sent = make_pair(rows, cols, steps)(xl_sent[0] if xl_sent else odd_sent, u, s_il, w)
        even = lax.ppermute(even_sent, axes, even_swap)
        part, sums = make_inner(rows, cols, steps)(u, r, s_il, s_xl, w)
        part, sums = make_near_edges(rows, cols, steps, n_il, n_xl, xl_parities)(
            u, r, s_il, s_xl, w, part, sums, even_sent, even, *xl_sent, *xl_got
        )
        image, row = make_edges(rows, cols, steps, n_il, n_dev)(u, r, s_il, w, part, sums, g, odd, g_got)
        rows_all = lax.all_to_all(row, axes, 0, 0, tiled=True)
        return make_update(rows, cols, steps)(rows_all, x, r, u, image)

    placed = P("il", "xl", None)
    return jax.shard_map(step, mesh=mesh, in_specs=(placed,) * 6, out_specs=(placed,) * 3, check_vma=False)
```
